32 devices in a mesh: ctx: 2 (over x), tp: 4 (over y, core), pp: 4 (over z).
Axes of the slice: x: 2, y: 2, z: 4, core: 2. Of those that a mesh axis runs over, the one named last changes fastest.
Arguments:
- lin_query: bfloat16 [4, 512, 8192], P('pp', 'ctx', 'tp'), may hold values from -6 to 6
- lin_key: bfloat16 [4, 512, 8192], P('pp', 'ctx', 'tp'), may hold values from -6 to 6
- lin_value: bfloat16 [4, 512, 8192], P('pp', 'ctx', 'tp'), may hold values from -6 to 6
- log_decay: float32 [4, 512, 64], P('pp', 'ctx', 'tp'), may hold values from -1 to 0, as said below
- out_gate: bfloat16 [4, 512, 8192], P('pp', 'ctx', 'tp'), may hold values from -6 to 6
- norm_gain: float32 [4, 8192], P('pp', 'tp'), may hold values from 0.1 to 1.9
- soft_query: bfloat16 [4, 512, 8192], P('pp', 'ctx', 'tp'), may hold values from -5 to 5
- soft_key: bfloat16 [4, 512, 1024], P('pp', 'ctx', 'tp'), may hold values from -5 to 5
- soft_value: bfloat16 [4, 512, 1024], P('pp', 'ctx', 'tp'), may hold values from -6 to 6
Outputs:
- lin_handed: bfloat16 [4, 512, 8192], P('pp', 'ctx', 'tp')
- soft_handed: bfloat16 [4, 512, 8192], P('pp', 'ctx', 'tp')
The draws below stay inside these ranges and needn't reach their ends.
Inputs may be any that keep to these rules, and one draw needn't show every extreme that they name: `log_decay`: negative everywhere.
All inputs are finite; a program needn't handle non-finite values.
Results may differ from the reference program's by a relative error of at most 0.0049.
Values may be sent and summed in bfloat16 or wider, within the bound.
No kernel may reach another device: no remote copies, remote signals or barrier semaphores. Data moves between devices by JAX's collectives and lax.ppermute only.
A program may use at most 128 MiB of HBM per device.

```python
import jax
import jax.numpy as jnp
from jax import lax

HEADS = 64
KV_HEADS = 8
HD = 128
BLK = 256
TOK_DEV = 256
MICRO_BATCHES = 4
SEQUENCE_LENGTH = 512
GROUP = 8


def draw_log_decay(key, part):
    flow_lanes = jax.random.split(key, 7)
    fast_share = 0.5
    fast_heads = jax.random.bernoulli(flow_lanes[0], fast_share, (MICRO_BATCHES, 1, HEADS))
    fast_rate = jax.random.uniform(flow_lanes[1], (MICRO_BATCHES, 1, HEADS), minval=0.045, maxval=0.08)
    slow_rate = -jnp.log(jax.random.uniform(flow_lanes[2], (MICRO_BATCHES, 1, HEADS), minval=0.5, maxval=0.8)) / SEQUENCE_LENGTH
    step_increment = jnp.where(fast_heads, fast_rate, slow_rate)
    shards = SEQUENCE_LENGTH // TOK_DEV
    accelerator_factor = jax.random.uniform(flow_lanes[3], (MICRO_BATCHES, shards, 1, HEADS), minval=0.6, maxval=1.5)
    accelerator_factor = jnp.broadcast_to(accelerator_factor, (MICRO_BATCHES, shards, TOK_DEV, HEADS)).reshape(MICRO_BATCHES, SEQUENCE_LENGTH, HEADS)
    element_factor = jax.random.uniform(flow_lanes[4], (MICRO_BATCHES, SEQUENCE_LENGTH, HEADS), minval=0.5, maxval=1.5)
    spike_events = jax.random.randint(flow_lanes[5], (MICRO_BATCHES, 1, 2), 0, SEQUENCE_LENGTH)
    placement_slots = jnp.arange(SEQUENCE_LENGTH)[None, :, None]
    hit_positions = jnp.any(placement_slots == spike_events, axis=-1)
    spike_logarithm = jnp.log(jax.random.uniform(flow_lanes[6], (MICRO_BATCHES, SEQUENCE_LENGTH, 1), minval=0.55, maxval=0.8))
    return -step_increment * accelerator_factor * element_factor + jnp.where(hit_positions[:, :, None], spike_logarithm, 0.0)


def draw_soft_query(key, part):
    draw_base = jnp.clip(jax.random.normal(jax.random.fold_in(key, 1), (MICRO_BATCHES, SEQUENCE_LENGTH, HEADS, HD)), -5.0, 5.0)
    return draw_base.reshape(MICRO_BATCHES, SEQUENCE_LENGTH, HEADS * HD).astype(jnp.bfloat16)


def draw_soft_key(key, part):
    draw_base = jnp.clip(jax.random.normal(jax.random.fold_in(key, 2), (MICRO_BATCHES, SEQUENCE_LENGTH, KV_HEADS, HD)), -5.0, 5.0)
    return draw_base.reshape(MICRO_BATCHES, SEQUENCE_LENGTH, KV_HEADS * HD).astype(jnp.bfloat16)


def steps_of(stream_key, dims, pieces, low, top_value):
    factor_of = 1.0
    for axis_at, shards_of in pieces:
        heights = jax.random.uniform(jax.random.fold_in(jax.random.fold_in(stream_key, 6), axis_at), (shards_of,), jnp.float32, low / len(pieces), top_value / len(pieces))
        factor_of = factor_of * jnp.repeat(jnp.exp(heights), dims[axis_at] // shards_of).reshape((-1,) + (1,) * (len(dims) - 1 - axis_at))
    return factor_of


def normal_values(rng, shape, width, reach, cuts=(), held_as=jnp.bfloat16):
    drawn = width * jax.random.normal(rng, shape, jnp.float32)
    if cuts:
        drawn = drawn * steps_of(rng, shape, cuts, -0.22, 0.18)
    return jnp.clip(drawn, -reach, reach).astype(held_as)


def setup_inputs(seed: int = 0) -> dict:
    key_list = jax.random.split(jax.random.key(seed), 10)
    return {
        "lin_query": normal_values(key_list[0], (MICRO_BATCHES, SEQUENCE_LENGTH, HEADS * HD), 1.0, 6.0, ((0, 4), (1, 2), (2, 4))),
        "lin_key": normal_values(key_list[1], (MICRO_BATCHES, SEQUENCE_LENGTH, HEADS * HD), 1.0, 6.0, ((0, 4), (1, 2), (2, 4))),
        "lin_value": normal_values(key_list[2], (MICRO_BATCHES, SEQUENCE_LENGTH, HEADS * HD), 1.0, 6.0, ((0, 4), (1, 2), (2, 4))),
        "log_decay": draw_log_decay(jax.random.fold_in(key_list[9], 71), 0),
        "out_gate": normal_values(key_list[4], (MICRO_BATCHES, SEQUENCE_LENGTH, HEADS * HD), 1.0, 6.0, ((0, 4), (1, 2), (2, 4))),
        "norm_gain": jnp.clip(1.0 + 0.18 * jax.random.normal(key_list[5], (MICRO_BATCHES, HEADS * HD), jnp.float32), 0.1, 1.9),
        "soft_query": draw_soft_query(jax.random.fold_in(key_list[9], 71), 0),
        "soft_key": draw_soft_key(jax.random.fold_in(key_list[9], 71), 0),
        "soft_value": normal_values(key_list[8], (MICRO_BATCHES, SEQUENCE_LENGTH, KV_HEADS * HD), 1.0, 6.0, ((0, 4), (1, 2), (2, 4))),
    }


epsilon = 1e-06
lowest = -1e+30

def lightning_segment(query_rows, key_rows, value_rows, decays, gate_rows, gain_row):
    blocks = SEQUENCE_LENGTH // BLK
    queries = query_rows.reshape(blocks, BLK, HEADS, HD)
    keys_all = key_rows.reshape(blocks, BLK, HEADS, HD)
    values_all = value_rows.reshape(blocks, BLK, HEADS, HD)
    decay_all = decays.reshape(blocks, BLK, HEADS)
    causal = (jnp.arange(BLK)[:, None] >= jnp.arange(BLK)[None, :])[None]

    def advance(state, inputs):
        query_blk, key_blk, value_blk, decay_blk = inputs
        running_log = jnp.cumsum(decay_blk, axis=0)
        closing_log = running_log[-1]
        scores = jnp.einsum('thd,shd->hts', query_blk.astype(jnp.float32), key_blk.astype(jnp.float32))
        log_gap = running_log.T[:, :, None] - running_log.T[:, None, :]
        decay_mask = jnp.where(causal, jnp.exp(jnp.where(causal, log_gap, 0.0)), 0.0)
        weights = (scores * decay_mask).astype(jnp.bfloat16)
        weights = lax.optimization_barrier(weights).astype(jnp.float32)
        inside = jnp.einsum('hts,shd->thd', weights, value_blk.astype(jnp.float32))
        lifted = query_blk.astype(jnp.float32) * jnp.exp(running_log)[:, :, None]
        earlier_part = jnp.einsum('thd,hde->the', lifted, state, precision=lax.Precision.HIGHEST)
        pressed = (key_blk.astype(jnp.float32) * jnp.exp(closing_log[None, :] - running_log)[:, :, None]).astype(jnp.bfloat16)
        pressed = lax.optimization_barrier(pressed).astype(jnp.float32)
        state = jnp.exp(closing_log)[:, None, None] * state + jnp.einsum('shd,she->hde', pressed, value_blk.astype(jnp.float32))
        return (state, inside + earlier_part)
    initial = jnp.zeros((HEADS, HD, HD), jnp.float32)
    _, mixture = lax.scan(advance, initial, (queries, keys_all, values_all, decay_all))
    mixture = mixture.reshape(SEQUENCE_LENGTH, HEADS, HD)
    normed = mixture * lax.rsqrt(lax.optimization_barrier(jnp.mean(mixture * mixture, axis=-1, keepdims=True)) + epsilon)
    gated = normed.reshape(SEQUENCE_LENGTH, HEADS * HD) * gain_row[None, :] * jax.nn.sigmoid(gate_rows.astype(jnp.float32))
    return gated.astype(jnp.bfloat16)

def softmax_segment(query_rows, key_rows, value_rows):
    tile_rows = min(128, SEQUENCE_LENGTH)
    queries = query_rows.reshape(SEQUENCE_LENGTH, KV_HEADS, GROUP, HD).astype(jnp.float32)
    keys_all = key_rows.reshape(SEQUENCE_LENGTH, KV_HEADS, HD).astype(jnp.float32)
    values_all = value_rows.reshape(SEQUENCE_LENGTH, KV_HEADS, HD).astype(jnp.float32)
    key_pos = jnp.arange(SEQUENCE_LENGTH)
    score_scale = HD ** (-0.5)

    def one_tile(first_row):
        rows_now = lax.dynamic_slice_in_dim(queries, first_row, tile_rows, 0)
        scores = jnp.einsum('tkgd,skd->tkgs', rows_now, keys_all) * score_scale
        row_pos = first_row + jnp.arange(tile_rows)
        causal = (row_pos[:, None] >= key_pos[None, :])[:, None, None, :]
        row_peak = lax.optimization_barrier(jnp.max(jnp.where(causal, scores, lowest), axis=-1, keepdims=True))
        unscaled = jnp.where(causal, jnp.exp(scores - row_peak), 0.0)
        totals = lax.optimization_barrier(jnp.sum(unscaled, axis=-1))
        rounded = lax.optimization_barrier(unscaled.astype(jnp.bfloat16)).astype(jnp.float32)
        weighted = jnp.einsum('tkgs,skd->tkgd', rounded, values_all)
        return (weighted / totals[..., None]).astype(jnp.bfloat16)
    starts = jnp.arange(SEQUENCE_LENGTH // tile_rows) * tile_rows
    tiles = lax.map(one_tile, starts)
    return tiles.reshape(SEQUENCE_LENGTH, HEADS * HD)

def reference(lin_query, lin_key, lin_value, log_decay, out_gate, norm_gain, soft_query, soft_key, soft_value):
    lin_list = []
    soft_list = []
    for segment_index in range(MICRO_BATCHES):
        lin_list.append(lightning_segment(lin_query[segment_index], lin_key[segment_index], lin_value[segment_index], log_decay[segment_index], out_gate[segment_index], norm_gain[segment_index]))
        soft_list.append(softmax_segment(soft_query[segment_index], soft_key[segment_index], soft_value[segment_index]))
    lin_out = jnp.stack(lin_list)
    soft_out = jnp.stack(soft_list)
    return (jnp.roll(lin_out, 1, axis=0), jnp.roll(soft_out, 1, axis=0))
```

```python
import functools

import jax
import jax.numpy as jnp
from jax import lax
from jax.experimental import pallas as pl
from jax.experimental.pallas import tpu as pltpu
from jax.sharding import PartitionSpec as P

HEADS = 64
KV_HEADS = 8
HD = 128
BLK = 256
GROUP = HEADS // KV_HEADS
HALF = BLK // 2

epsilon = 1e-06
lowest = -1e30
LOG2E = 1.4426950408889634
MIB = 1 << 20


def passed_along(block, axis, distance):
    devices = lax.axis_size(axis)
    return lax.ppermute(block, axis, [((i - distance) % devices, i) for i in range(devices)])


def running_sums(decay_rows):
    total = decay_rows
    place = lax.broadcasted_iota(jnp.int32, total.shape, 1)
    reach = 1
    while reach < total.shape[1]:
        total = total + jnp.where(place >= reach, pltpu.roll(total, reach, 1), 0.0)
        reach *= 2
    return total


def turned(rows):
    fill = jnp.zeros((HD - rows.shape[0], rows.shape[1]), rows.dtype)
    return jnp.transpose(jnp.concatenate([rows, fill], axis=0))


def states_kernel(key_ref, value_ref, decay_ref, state_ref):
    running = running_sums(decay_ref[0])
    press = turned(jnp.exp(running[:, BLK - 1 :] - running))
    for h in range(state_ref.shape[0]):
        lanes = slice(h * HD, (h + 1) * HD)
        pressed = (key_ref[0, :, lanes].astype(jnp.float32) * press[:, h : h + 1]).astype(jnp.bfloat16)
        state_ref[h] = lax.dot_general(
            pressed, value_ref[0, :, lanes], (((0,), (0,)), ((), ())), preferred_element_type=jnp.float32
        ).astype(state_ref.dtype)


def closing_states(lin_key, lin_value, decay_rows, part, parts):
    heads = decay_rows.shape[1] // parts
    wide = pl.BlockSpec((1, BLK, heads * HD), lambda i: (0, 0, part))
    return pl.pallas_call(
        states_kernel,
        grid=(1,),
        in_specs=[wide, wide, pl.BlockSpec((1, heads, BLK), lambda i: (0, part, 0))],
        out_specs=pl.BlockSpec((heads, HD, HD), lambda i: (0, 0, 0)),
        out_shape=jax.ShapeDtypeStruct((heads, HD, HD), jnp.bfloat16),
        compiler_params=pltpu.CompilerParams(vmem_limit_bytes=16 * MIB),
        name="closing_states",
    )(lin_key, lin_value, decay_rows)


def mix_kernel(query_ref, key_ref, value_ref, decay_ref, gate_ref, gain_ref, state_ref, out_ref):
    running = running_sums(decay_ref[0])
    columns = turned(running)
    lift = jnp.exp(columns)
    causal = lax.broadcasted_iota(jnp.int32, (HALF, HALF), 0) >= lax.broadcasted_iota(
        jnp.int32, (HALF, HALF), 1
    )
    turned_dims = (((1,), (1,)), ((), ()))
    for h in range(state_ref.shape[0]):
        lanes = slice(h * HD, (h + 1) * HD)
        queries = query_ref[0, :, lanes]
        keys = key_ref[0, :, lanes]
        values = value_ref[0, :, lanes]
        column = columns[:, h : h + 1]
        row = running[h : h + 1, :]
        earlier = jnp.dot(queries, state_ref[h], preferred_element_type=jnp.float32) * lift[:, h : h + 1]
        parts = []
        for b in range(2):
            rows = slice(b * HALF, (b + 1) * HALF)
            seen = (b + 1) * HALF
            scores = lax.dot_general(
                queries[rows], keys[:seen], turned_dims, preferred_element_type=jnp.float32
            )
            pieces = []
            for c in range(b + 1):
                span = slice(c * HALF, (c + 1) * HALF)
                gap = column[rows] - row[:, span]
                if c == b:
                    fall = jnp.where(causal, jnp.exp(jnp.where(causal, gap, 0.0)), 0.0)
                else:
                    fall = jnp.exp(gap)
                pieces.append((scores[:, span] * fall).astype(jnp.bfloat16))
            weights = pieces[0] if b == 0 else jnp.concatenate(pieces, axis=1)
            parts.append(jnp.dot(weights, values[:seen], preferred_element_type=jnp.float32))
        mixture = jnp.concatenate(parts, axis=0) + earlier
        scale = lax.rsqrt(jnp.mean(mixture * mixture, axis=1, keepdims=True) + epsilon)
        gate = jax.nn.sigmoid(gate_ref[0, :, lanes].astype(jnp.float32))
        out_ref[0, :, lanes] = (mixture * scale * gain_ref[0:1, lanes] * gate).astype(out_ref.dtype)


def lightning(lin_query, lin_key, lin_value, decay_rows, out_gate, norm_gain, incoming, part, parts):
    heads = decay_rows.shape[1] // parts
    wide = pl.BlockSpec((1, BLK, heads * HD), lambda i: (0, 0, part))
    return pl.pallas_call(
        mix_kernel,
        grid=(1,),
        in_specs=[
            wide,
            wide,
            wide,
            pl.BlockSpec((1, heads, BLK), lambda i: (0, part, 0)),
            wide,
            pl.BlockSpec((1, heads * HD), lambda i: (0, part)),
            pl.BlockSpec((heads, HD, HD), lambda i: (0, 0, 0)),
        ],
        out_specs=pl.BlockSpec((1, BLK, heads * HD), lambda i: (0, 0, 0)),
        out_shape=jax.ShapeDtypeStruct((1, BLK, heads * HD), jnp.bfloat16),
        compiler_params=pltpu.CompilerParams(vmem_limit_bytes=20 * MIB),
        name="lightning_mix",
    )(lin_query, lin_key, lin_value, decay_rows, out_gate, norm_gain, incoming)


def pack_kernel(query_ref, key_ref, value_ref, raw_ref, *refs):
    pair_refs, sems = refs[:-1], refs[-1]
    width = GROUP * HD
    copies = [
        (key_ref.at[:, :, pl.ds(0, HD)], raw_ref.at[:, :, pl.ds(width, HD)]),
        (value_ref.at[:, :, pl.ds(0, HD)], raw_ref.at[:, :, pl.ds(width + HD, HD)]),
        (query_ref.at[:, :, pl.ds(0, width)], raw_ref.at[:, :, pl.ds(0, width)]),
    ]
    for i, pair_ref in enumerate(pair_refs):
        lanes = pl.ds((i + 1) * HD, HD)
        copies.append((key_ref.at[:, :, lanes], pair_ref.at[:, :, pl.ds(0, HD)]))
        copies.append((value_ref.at[:, :, lanes], pair_ref.at[:, :, pl.ds(HD, HD)]))
    started = [pltpu.make_async_copy(a, b, sems.at[i]) for i, (a, b) in enumerate(copies)]
    for copy in started:
        copy.start()
    for copy in started:
        copy.wait()


def packed(soft_query, soft_key, soft_value):
    kv_count = soft_key.shape[2] // HD
    in_hbm = pl.BlockSpec(memory_space=pltpu.HBM)
    in_vmem = pl.BlockSpec(memory_space=pltpu.VMEM)
    widths = [(GROUP + 2) * HD] + [2 * HD] * (kv_count - 1)
    return pl.pallas_call(
        pack_kernel,
        in_specs=[in_hbm] * 3,
        out_specs=[in_vmem] * kv_count,
        out_shape=[jax.ShapeDtypeStruct((1, BLK, width), jnp.bfloat16) for width in widths],
        scratch_shapes=[pltpu.SemaphoreType.DMA((1 + 2 * kv_count,))],
        compiler_params=pltpu.CompilerParams(vmem_limit_bytes=60 * MIB),
        name="packed",
    )(soft_query, soft_key, soft_value)


def attend(place, query_ref, key_ref, value_ref, before_ref, out_ref):
    others = before_ref.shape[0]
    factor = HD ** (-0.5) * LOG2E
    causal = lax.broadcasted_iota(jnp.int32, (BLK, BLK), 0) >= lax.broadcasted_iota(jnp.int32, (BLK, BLK), 1)
    turned_dims = (((1,), (1,)), ((), ()))
    keys, values = slice(0, HD), slice(HD, 2 * HD)

    def scored(queries, keys):
        return lax.dot_general(queries, keys, turned_dims, preferred_element_type=jnp.float32)

    for h in range(GROUP):
        lanes = slice(h * HD, (h + 1) * HD)
        queries = query_ref[0, :, lanes]
        own = jnp.where(causal, scored(queries, key_ref[0]), lowest)
        peak = jnp.max(own, axis=1, keepdims=True)
        if others == 1:
            before = jnp.where(place > 0, scored(queries, before_ref[0, :, keys]), lowest)
            peak = jnp.maximum(peak, jnp.max(before, axis=1, keepdims=True))
            own = jnp.exp2((own - peak) * factor)
            before = jnp.exp2((before - peak) * factor)
            totals = jnp.sum(own, axis=1, keepdims=True) + jnp.sum(before, axis=1, keepdims=True)
            weighted = jnp.dot(
                own.astype(jnp.bfloat16), value_ref[0], preferred_element_type=jnp.float32
            ) + jnp.dot(
                before.astype(jnp.bfloat16), before_ref[0, :, values], preferred_element_type=jnp.float32
            )
        else:
            own = jnp.exp2((own - peak) * factor)
            totals = jnp.sum(own, axis=1, keepdims=True)
            weighted = jnp.dot(
                own.astype(jnp.bfloat16), value_ref[0], preferred_element_type=jnp.float32
            )

            def absorb(turn, kept):
                peak, totals, weighted = kept
                scores = scored(queries, before_ref[turn, :, keys])
                new_peak = jnp.maximum(peak, jnp.max(scores, axis=1, keepdims=True))
                shrink = jnp.exp2((peak - new_peak) * factor)
                scores = jnp.exp2((scores - new_peak) * factor)
                totals = totals * shrink + jnp.sum(scores, axis=1, keepdims=True)
                weighted = weighted * shrink + jnp.dot(
                    scores.astype(jnp.bfloat16),
                    before_ref[turn, :, values],
                    preferred_element_type=jnp.float32,
                )
                return (new_peak, totals, weighted)

            peak, totals, weighted = lax.fori_loop(0, place, absorb, (peak, totals, weighted))
        out_ref[0, :, lanes] = (weighted / totals).astype(out_ref.dtype)


def soft_kernel(place_ref, query_ref, key_ref, value_ref, before_ref, out_ref):
    attend(place_ref[0], query_ref, key_ref, value_ref, before_ref, out_ref)


def soft_cost(others):
    return pl.CostEstimate(
        flops=4 * GROUP * BLK * BLK * (others + 1) * HD,
        bytes_accessed=5 * GROUP * BLK * HD,
        transcendentals=GROUP * BLK * BLK * (others + 1),
    )


def softmax_group(place, soft_query, pair, before, group):
    others = before.shape[0]
    wide = (1, BLK, GROUP * HD)
    return pl.pallas_call(
        soft_kernel,
        grid_spec=pltpu.PrefetchScalarGridSpec(
            num_scalar_prefetch=1,
            grid=(1,),
            in_specs=[
                pl.BlockSpec(wide, lambda i, place: (0, 0, group)),
                pl.BlockSpec((1, BLK, HD), lambda i, place: (0, 0, 0)),
                pl.BlockSpec((1, BLK, HD), lambda i, place: (0, 0, 1)),
                pl.BlockSpec((others, BLK, 2 * HD), lambda i, place: (0, 0, 0)),
            ],
            out_specs=pl.BlockSpec(wide, lambda i, place: (0, 0, 0)),
        ),
        out_shape=jax.ShapeDtypeStruct(wide, jnp.bfloat16),
        compiler_params=pltpu.CompilerParams(vmem_limit_bytes=20 * MIB),
        name="softmax_group",
    )(place, soft_query, pair, pair, before)


def finish_kernel(place_ref, query_ref, key_ref, value_ref, before_ref, ready_ref, out_ref):
    @pl.when(pl.program_id(0) == 0)
    def _():
        attend(place_ref[0], query_ref, key_ref, value_ref, before_ref, out_ref)

    @pl.when(pl.program_id(0) > 0)
    def _():
        out_ref[...] = ready_ref[...]


def softmax_finish(place, raw, before, ready):
    others = before.shape[0]
    wide = (1, BLK, GROUP * HD)
    groups = 1 + ready.shape[2] // (GROUP * HD)
    return pl.pallas_call(
        finish_kernel,
        grid_spec=pltpu.PrefetchScalarGridSpec(
            num_scalar_prefetch=1,
            grid=(groups,),
            in_specs=[
                pl.BlockSpec(wide, lambda i, place: (0, 0, 0)),
                pl.BlockSpec((1, BLK, HD), lambda i, place: (0, 0, GROUP)),
                pl.BlockSpec((1, BLK, HD), lambda i, place: (0, 0, GROUP + 1)),
                pl.BlockSpec((others, BLK, 2 * HD), lambda i, place: (0, 0, 0)),
                pl.BlockSpec(wide, lambda i, place: (0, 0, jnp.maximum(i - 1, 0))),
            ],
            out_specs=pl.BlockSpec(wide, lambda i, place: (0, 0, i)),
        ),
        out_shape=jax.ShapeDtypeStruct((1, BLK, groups * GROUP * HD), jnp.bfloat16),
        compiler_params=pltpu.CompilerParams(vmem_limit_bytes=20 * MIB),
        name="softmax_finish",
    )(place, raw, raw, raw, before, ready)


def place_kernel(part, block_ref, *refs):
    whole_ref, sem = refs[-2:]
    width = block_ref.shape[2]
    copy = pltpu.make_async_copy(block_ref, whole_ref.at[:, :, pl.ds(part * width, width)], sem)
    copy.start()
    copy.wait()


def placed(block, part, parts, whole=None):
    anywhere = pl.BlockSpec(memory_space=pl.ANY)
    operands = (block,) if whole is None else (block, whole)
    return pl.pallas_call(
        functools.partial(place_kernel, part),
        in_specs=[anywhere] * len(operands),
        out_specs=anywhere,
        out_shape=jax.ShapeDtypeStruct(block.shape[:2] + (parts * block.shape[2],), block.dtype),
        scratch_shapes=[pltpu.SemaphoreType.DMA],
        input_output_aliases={} if whole is None else {1: 0},
        compiler_params=pltpu.CompilerParams(vmem_limit_bytes=1 * MIB),
        name="placed",
    )(*operands)


def earlier_blocks(block):
    devices = lax.axis_size("ctx")
    if devices == 2:
        return lax.ppermute(block, "ctx", [(0, 1)])
    return lax.all_gather(block, "ctx", axis=0, tiled=True)[: devices - 1]


def incoming_states(closing, decay_rows):
    if lax.axis_size("ctx") == 2:
        return lax.ppermute(closing, "ctx", [(0, 1)])
    states = lax.all_gather(closing[None], "ctx", axis=0, tiled=True)
    logs = lax.all_gather(jnp.sum(decay_rows, axis=2), "ctx", axis=0, tiled=True)
    earlier = (lax.iota(jnp.int32, logs.shape[0]) < lax.axis_index("ctx"))[:, None]
    reached = jnp.sum(jnp.where(earlier, logs, 0.0), axis=0)
    rising = jnp.cumsum(logs, axis=0)
    weight = jnp.where(earlier, jnp.exp(jnp.where(earlier, reached[None, :] - rising, 0.0)), 0.0)
    return jnp.sum(weight[:, :, None, None] * states.astype(jnp.float32), axis=0).astype(jnp.bfloat16)


PARTS = 2


def local(
    lin_query, lin_key, lin_value, log_decay, out_gate, norm_gain, soft_query, soft_key, soft_value
):
    place = lax.axis_index("ctx").astype(jnp.int32)[None]
    decay_rows = jnp.swapaxes(log_decay, 1, 2)
    heads = decay_rows.shape[1] // PARTS
    raw, *pairs = packed(soft_query, soft_key, soft_value)
    handed_raw = passed_along(raw, "pp", 1)
    befores = [earlier_blocks(pair) for pair in pairs]
    ready = [
        passed_along(softmax_group(place, soft_query, pair, before, g + 1), "pp", 1)
        for g, (pair, before) in enumerate(zip(pairs, befores))
    ]
    ready = ready[0] if len(ready) == 1 else jnp.concatenate(ready, axis=2)
    lin_key, lin_value, *befores = lax.optimization_barrier((lin_key, lin_value, *befores))
    incoming = []
    for part in range(PARTS):
        closing = closing_states(lin_key, lin_value, decay_rows, part, PARTS)
        incoming.append(incoming_states(closing, decay_rows[:, part * heads : (part + 1) * heads]))
    incoming[0], handed_raw = lax.optimization_barrier((incoming[0], handed_raw))
    lin_parts = [
        passed_along(
            lightning(
                lin_query, lin_key, lin_value, decay_rows, out_gate, norm_gain, incoming[part], part, PARTS
            ),
            "pp",
            1,
        )
        for part in range(PARTS)
    ]
    before = earlier_blocks(handed_raw[:, :, GROUP * HD :])
    soft_handed = softmax_finish(place, handed_raw, before, ready)
    lin_handed = None
    for part in range(PARTS):
        lin_handed = placed(lin_parts[part], part, PARTS, lin_handed)
    return (lin_handed, soft_handed)


def solution(mesh):
    wide = P("pp", "ctx", "tp")
    return jax.shard_map(
        local,
        mesh=mesh,
        in_specs=(wide, wide, wide, wide, wide, P("pp", "tp"), wide, wide, wide),
        out_specs=(wide, wide),
        check_vma=False,
    )
```

```python
import functools

import jax
import jax.numpy as jnp
from jax import lax
from jax.experimental import pallas as pl
from jax.experimental.pallas import tpu as pltpu
from jax.sharding import PartitionSpec as P

HEADS = 64
KV_HEADS = 8
HD = 128
BLK = 256
GROUP = HEADS // KV_HEADS
HALF = BLK // 2

epsilon = 1e-06
lowest = -1e30
LOG2E = 1.4426950408889634
MIB = 1 << 20


def passed_along(block, axis, distance):
    devices = lax.axis_size(axis)
    return lax.ppermute(block, axis, [((i - distance) % devices, i) for i in range(devices)])


def running_sums(decay_rows):
    total = decay_rows
    place = lax.broadcasted_iota(jnp.int32, total.shape, 1)
    reach = 1
    while reach < total.shape[1]:
        total = total + jnp.where(place >= reach, pltpu.roll(total, reach, 1), 0.0)
        reach *= 2
    return total


def turned(rows):
    fill = jnp.zeros((HD - rows.shape[0], rows.shape[1]), rows.dtype)
    return jnp.transpose(jnp.concatenate([rows, fill], axis=0))


def states_kernel(key_ref, value_ref, decay_ref, state_ref):
    running = running_sums(decay_ref[0])
    press = turned(jnp.exp(running[:, BLK - 1 :] - running))
    for h in range(state_ref.shape[0]):
        lanes = slice(h * HD, (h + 1) * HD)
        pressed = (key_ref[0, :, lanes].astype(jnp.float32) * press[:, h : h + 1]).astype(jnp.bfloat16)
        state_ref[h] = lax.dot_general(
            pressed, value_ref[0, :, lanes], (((0,), (0,)), ((), ())), preferred_element_type=jnp.float32
        ).astype(state_ref.dtype)


def closing_states(lin_key, lin_value, decay_rows, part, parts):
    heads = decay_rows.shape[1] // parts
    wide = pl.BlockSpec((1, BLK, heads * HD), lambda i: (0, 0, part))
    return pl.pallas_call(
        states_kernel,
        grid=(1,),
        in_specs=[wide, wide, pl.BlockSpec((1, heads, BLK), lambda i: (0, part, 0))],
        out_specs=pl.BlockSpec((heads, HD, HD), lambda i: (0, 0, 0)),
        out_shape=jax.ShapeDtypeStruct((heads, HD, HD), jnp.bfloat16),
        compiler_params=pltpu.CompilerParams(vmem_limit_bytes=16 * MIB),
        name="closing_states",
    )(lin_key, lin_value, decay_rows)


def mix_kernel(place_ref, query_ref, key_ref, value_ref, decay_ref, gate_ref, gain_ref, state_ref, *out_refs):
    running = running_sums(decay_ref[0])
    columns = turned(running)
    lift = jnp.exp(columns)
    causal = lax.broadcasted_iota(jnp.int32, (HALF, HALF), 0) >= lax.broadcasted_iota(
        jnp.int32, (HALF, HALF), 1
    )
    turned_dims = (((1,), (1,)), ((), ()))
    owner = []
    for out_ref in out_refs:
        first = len(owner)
        owner += [(out_ref, first)] * (out_ref.shape[2] // HD)
    for h in range(state_ref.shape[0]):
        lanes = slice(h * HD, (h + 1) * HD)
        queries = query_ref[0, :, lanes]
        keys = key_ref[0, :, lanes]
        values = value_ref[0, :, lanes]
        column = columns[:, h : h + 1]
        row = running[h : h + 1, :]
        earlier = jnp.dot(queries, state_ref[h], preferred_element_type=jnp.float32) * lift[:, h : h + 1]
        earlier = jnp.where(place_ref[0] > 0, earlier, 0.0)
        parts = []
        for b in range(2):
            rows = slice(b * HALF, (b + 1) * HALF)
            seen = (b + 1) * HALF
            scores = lax.dot_general(
                queries[rows], keys[:seen], turned_dims, preferred_element_type=jnp.float32
            )
            pieces = []
            for c in range(b + 1):
                span = slice(c * HALF, (c + 1) * HALF)
                gap = column[rows] - row[:, span]
                if c == b:
                    fall = jnp.where(causal, jnp.exp(jnp.where(causal, gap, 0.0)), 0.0)
                else:
                    fall = jnp.exp(gap)
                pieces.append((scores[:, span] * fall).astype(jnp.bfloat16))
            weights = pieces[0] if b == 0 else jnp.concatenate(pieces, axis=1)
            parts.append(jnp.dot(weights, values[:seen], preferred_element_type=jnp.float32))
        mixture = jnp.concatenate(parts, axis=0) + earlier
        scale = lax.rsqrt(jnp.mean(mixture * mixture, axis=1, keepdims=True) + epsilon)
        gate = jax.nn.sigmoid(gate_ref[0, :, lanes].astype(jnp.float32))
        result = mixture * scale * gain_ref[0:1, lanes] * gate
        out_ref, first = owner[h]
        lanes = slice((h - first) * HD, (h - first + 1) * HD)
        out_ref[0, :, lanes] = result.astype(out_ref.dtype)


def lightning(
    place, lin_query, lin_key, lin_value, decay_rows, out_gate, norm_gain, incoming, part, parts, chunks
):
    heads = decay_rows.shape[1] // parts
    wide = pl.BlockSpec((1, BLK, heads * HD), lambda i, place: (0, 0, part))
    return pl.pallas_call(
        mix_kernel,
        grid_spec=pltpu.PrefetchScalarGridSpec(
            num_scalar_prefetch=1,
            grid=(1,),
            in_specs=[
                wide,
                wide,
                wide,
                pl.BlockSpec((1, heads, BLK), lambda i, place: (0, part, 0)),
                wide,
                pl.BlockSpec((1, heads * HD), lambda i, place: (0, part)),
                pl.BlockSpec((heads, HD, HD), lambda i, place: (0, 0, 0)),
            ],
            out_specs=[pl.BlockSpec((1, BLK, n * HD), lambda i, place: (0, 0, 0)) for n in chunks],
        ),
        out_shape=[jax.ShapeDtypeStruct((1, BLK, n * HD), jnp.bfloat16) for n in chunks],
        compiler_params=pltpu.CompilerParams(vmem_limit_bytes=20 * MIB),
        name="lightning_mix",
    )(place, lin_query, lin_key, lin_value, decay_rows, out_gate, norm_gain, incoming)


def copied(pieces, sems):
    copies = [pltpu.make_async_copy(a, b, sems.at[i]) for i, (a, b) in enumerate(pieces)]
    for copy in copies:
        copy.start()
    for copy in copies:
        copy.wait()


def pack_kernel(query_ref, key_ref, value_ref, raw_ref, *refs):
    width = GROUP * HD
    pieces = [
        (query_ref.at[:, :, pl.ds(0, width)], raw_ref.at[:, :, pl.ds(0, width)]),
        (key_ref.at[:, :, pl.ds(0, HD)], raw_ref.at[:, :, pl.ds(width, HD)]),
        (value_ref.at[:, :, pl.ds(0, HD)], raw_ref.at[:, :, pl.ds(width + HD, HD)]),
    ]
    for i, pair_ref in enumerate(refs[:-1]):
        lanes = pl.ds((i + 1) * HD, HD)
        pieces.append((key_ref.at[:, :, lanes], pair_ref.at[:, :, pl.ds(0, HD)]))
        pieces.append((value_ref.at[:, :, lanes], pair_ref.at[:, :, pl.ds(HD, HD)]))
    copied(pieces, refs[-1])


def packed(soft_query, soft_key, soft_value):
    kv_count = soft_key.shape[2] // HD
    widths = [(GROUP + 2) * HD] + [2 * HD] * (kv_count - 1)
    return pl.pallas_call(
        pack_kernel,
        in_specs=[pl.BlockSpec(memory_space=pltpu.HBM)] * 3,
        out_specs=[pl.BlockSpec(memory_space=pltpu.VMEM)] * kv_count,
        out_shape=[pltpu.VMEM((1, BLK, width), jnp.bfloat16) for width in widths],
        scratch_shapes=[pltpu.SemaphoreType.DMA((1 + 2 * kv_count,))],
        compiler_params=pltpu.CompilerParams(vmem_limit_bytes=4 * MIB),
        name="packed",
    )(soft_query, soft_key, soft_value)


def attend(place, query_ref, key_ref, value_ref, before_ref, out_ref):
    others = before_ref.shape[0]
    factor = HD ** (-0.5) * LOG2E
    causal = lax.broadcasted_iota(jnp.int32, (BLK, BLK), 0) >= lax.broadcasted_iota(jnp.int32, (BLK, BLK), 1)
    turned_dims = (((1,), (1,)), ((), ()))
    keys, values = slice(0, HD), slice(HD, 2 * HD)

    def scored(queries, keys):
        return lax.dot_general(queries, keys, turned_dims, preferred_element_type=jnp.float32)

    for h in range(query_ref.shape[2] // HD):
        lanes = slice(h * HD, (h + 1) * HD)
        queries = query_ref[0, :, lanes]
        own = jnp.where(causal, scored(queries, key_ref[0]), lowest)
        peak = jnp.max(own, axis=1, keepdims=True)
        if others == 1:
            before = jnp.where(place > 0, scored(queries, before_ref[0, :, keys]), lowest)
            peak = jnp.maximum(peak, jnp.max(before, axis=1, keepdims=True))
            own = jnp.exp2((own - peak) * factor)
            before = jnp.exp2((before - peak) * factor)
            totals = jnp.sum(own, axis=1, keepdims=True) + jnp.sum(before, axis=1, keepdims=True)
            weighted = jnp.dot(
                own.astype(jnp.bfloat16), value_ref[0], preferred_element_type=jnp.float32
            ) + jnp.dot(
                before.astype(jnp.bfloat16), before_ref[0, :, values], preferred_element_type=jnp.float32
            )
        else:
            own = jnp.exp2((own - peak) * factor)
            totals = jnp.sum(own, axis=1, keepdims=True)
            weighted = jnp.dot(
                own.astype(jnp.bfloat16), value_ref[0], preferred_element_type=jnp.float32
            )

            def absorb(turn, kept):
                peak, totals, weighted = kept
                scores = scored(queries, before_ref[turn, :, keys])
                new_peak = jnp.maximum(peak, jnp.max(scores, axis=1, keepdims=True))
                shrink = jnp.exp2((peak - new_peak) * factor)
                scores = jnp.exp2((scores - new_peak) * factor)
                totals = totals * shrink + jnp.sum(scores, axis=1, keepdims=True)
                weighted = weighted * shrink + jnp.dot(
                    scores.astype(jnp.bfloat16),
                    before_ref[turn, :, values],
                    preferred_element_type=jnp.float32,
                )
                return (new_peak, totals, weighted)

            peak, totals, weighted = lax.fori_loop(0, place, absorb, (peak, totals, weighted))
        out_ref[0, :, lanes] = (weighted / totals).astype(out_ref.dtype)


def soft_kernel(place_ref, query_ref, key_ref, value_ref, before_ref, out_ref):
    attend(place_ref[0], query_ref, key_ref, value_ref, before_ref, out_ref)


STEP = 8


def softmax_group(place, soft_query, pair, before, group):
    others = before.shape[0]
    steps = GROUP // STEP
    wide = (1, BLK, STEP * HD)
    return pl.pallas_call(
        soft_kernel,
        grid_spec=pltpu.PrefetchScalarGridSpec(
            num_scalar_prefetch=1,
            grid=(steps,),
            in_specs=[
                pl.BlockSpec(wide, lambda i, place: (0, 0, group * steps + i)),
                pl.BlockSpec((1, BLK, HD), lambda i, place: (0, 0, 0)),
                pl.BlockSpec((1, BLK, HD), lambda i, place: (0, 0, 1)),
                pl.BlockSpec((others, BLK, 2 * HD), lambda i, place: (0, 0, 0)),
            ],
            out_specs=pl.BlockSpec(wide, lambda i, place: (0, 0, i)),
        ),
        out_shape=jax.ShapeDtypeStruct((1, BLK, GROUP * HD), jnp.bfloat16),
        compiler_params=pltpu.CompilerParams(vmem_limit_bytes=20 * MIB),
        name="softmax_group",
    )(place, soft_query, pair, pair, before)


def finish_kernel(place_ref, query_ref, key_ref, value_ref, before_ref, ready_ref, out_ref):
    here = pl.program_id(0) < GROUP // STEP

    @pl.when(here)
    def _():
        attend(place_ref[0], query_ref, key_ref, value_ref, before_ref, out_ref)

    @pl.when(jnp.logical_not(here))
    def _():
        out_ref[...] = ready_ref[...]


def softmax_finish(place, raw, before, ready):
    others = before.shape[0]
    steps = GROUP // STEP
    wide = (1, BLK, STEP * HD)
    groups = 1 + ready.shape[2] // (GROUP * HD)
    return pl.pallas_call(
        finish_kernel,
        grid_spec=pltpu.PrefetchScalarGridSpec(
            num_scalar_prefetch=1,
            grid=(groups * steps,),
            in_specs=[
                pl.BlockSpec(wide, lambda i, place: (0, 0, jnp.minimum(i, steps - 1))),
                pl.BlockSpec((1, BLK, HD), lambda i, place: (0, 0, GROUP)),
                pl.BlockSpec((1, BLK, HD), lambda i, place: (0, 0, GROUP + 1)),
                pl.BlockSpec((others, BLK, 2 * HD), lambda i, place: (0, 0, 0)),
                pl.BlockSpec(wide, lambda i, place: (0, 0, jnp.maximum(i - steps, 0))),
            ],
            out_specs=pl.BlockSpec(wide, lambda i, place: (0, 0, i)),
        ),
        out_shape=jax.ShapeDtypeStruct((1, BLK, groups * GROUP * HD), jnp.bfloat16),
        compiler_params=pltpu.CompilerParams(vmem_limit_bytes=20 * MIB),
        name="softmax_finish",
    )(place, raw, raw, raw, before, ready)


def place_kernel(start, block_ref, *refs):
    whole_ref, sems = refs[-2:]
    copied([(block_ref, whole_ref.at[:, :, pl.ds(start, block_ref.shape[2])])], sems)


def placed(block, start, width, whole=None):
    anywhere = pl.BlockSpec(memory_space=pl.ANY)
    operands = (block,) if whole is None else (block, whole)
    return pl.pallas_call(
        functools.partial(place_kernel, start),
        in_specs=[anywhere] * len(operands),
        out_specs=anywhere,
        out_shape=jax.ShapeDtypeStruct(block.shape[:2] + (width,), block.dtype),
        scratch_shapes=[pltpu.SemaphoreType.DMA((1,))],
        input_output_aliases={} if whole is None else {1: 0},
        compiler_params=pltpu.CompilerParams(vmem_limit_bytes=1 * MIB),
        name="placed",
    )(*operands)


def earlier_blocks(block):
    devices = lax.axis_size("ctx")
    if devices == 2:
        return passed_along(block, "ctx", 1)
    return lax.all_gather(block, "ctx", axis=0, tiled=True)[: devices - 1]


def incoming_states(closing, decay_rows):
    if lax.axis_size("ctx") == 2:
        return passed_along(closing, "ctx", 1)
    states = lax.all_gather(closing[None], "ctx", axis=0, tiled=True)
    logs = lax.all_gather(jnp.sum(decay_rows, axis=2), "ctx", axis=0, tiled=True)
    earlier = (lax.iota(jnp.int32, logs.shape[0]) < lax.axis_index("ctx"))[:, None]
    reached = jnp.sum(jnp.where(earlier, logs, 0.0), axis=0)
    rising = jnp.cumsum(logs, axis=0)
    weight = jnp.where(earlier, jnp.exp(jnp.where(earlier, reached[None, :] - rising, 0.0)), 0.0)
    return jnp.sum(weight[:, :, None, None] * states.astype(jnp.float32), axis=0).astype(jnp.bfloat16)


PARTS = 2
LAST = 2


def local(
    lin_query, lin_key, lin_value, log_decay, out_gate, norm_gain, soft_query, soft_key, soft_value
):
    place = lax.axis_index("ctx").astype(jnp.int32)[None]
    lin_query, lin_key, lin_value, out_gate, soft_query, soft_key, soft_value = (
        pltpu.with_memory_space_constraint(x, pltpu.HBM)
        for x in (lin_query, lin_key, lin_value, out_gate, soft_query, soft_key, soft_value)
    )
    decay_rows = jnp.swapaxes(log_decay, 1, 2)
    heads = decay_rows.shape[1] // PARTS
    raw, *pairs = packed(soft_query, soft_key, soft_value)
    handed_raw = passed_along(raw, "pp", 1)
    befores = [earlier_blocks(pair) for pair in pairs]
    lin_key, lin_value, raw = lax.optimization_barrier((lin_key, lin_value, raw))
    closing = [closing_states(lin_key, lin_value, decay_rows, part, PARTS) for part in range(PARTS)]
    closing[0], *befores = lax.optimization_barrier((closing[0], *befores))
    ready = [
        softmax_group(place, soft_query, pair, before, g + 1)
        for g, (pair, before) in enumerate(zip(pairs, befores))
    ]
    incoming = [
        incoming_states(closing[part], decay_rows[:, part * heads : (part + 1) * heads])
        for part in range(PARTS)
    ]
    ready = [passed_along(group, "pp", 1) for group in ready]
    ready = ready[0] if len(ready) == 1 else jnp.concatenate(ready, axis=2)
    incoming[0], handed_raw = lax.optimization_barrier((incoming[0], handed_raw))
    chunks = []
    for part in range(PARTS):
        chunks += lightning(
            place,
            lin_query,
            lin_key,
            lin_value,
            decay_rows,
            out_gate,
            norm_gain,
            incoming[part],
            part,
            PARTS,
            [heads - LAST, LAST] if part == PARTS - 1 else [heads],
        )
    chunks = [passed_along(chunk, "pp", 1) for chunk in chunks]
    before = earlier_blocks(handed_raw[:, :, GROUP * HD :])
    soft_handed = softmax_finish(place, handed_raw, before, ready)
    lin_handed = None
    start = 0
    for chunk in chunks:
        lin_handed = placed(chunk, start, lin_query.shape[2], lin_handed)
        start += chunk.shape[2]
    return (lin_handed, soft_handed)


def solution(mesh):
    wide = P("pp", "ctx", "tp")
    return jax.shard_map(
        local,
        mesh=mesh,
        in_specs=(wide, wide, wide, wide, wide, P("pp", "tp"), wide, wide, wide),
        out_specs=(wide, wide),
        check_vma=False,
    )
```

```python
import functools

import jax
import jax.numpy as jnp
from jax import lax
from jax.experimental import pallas as pl
from jax.experimental.pallas import tpu as pltpu
from jax.sharding import PartitionSpec as P

HEADS = 64
KV_HEADS = 8
HD = 128
BLK = 256
GROUP = HEADS // KV_HEADS
HALF = BLK // 2

epsilon = 1e-06
lowest = -1e30
LOG2E = 1.4426950408889634
MIB = 1 << 20


def passed_along(block, axis, distance):
    devices = lax.axis_size(axis)
    return lax.ppermute(block, axis, [((i - distance) % devices, i) for i in range(devices)])


def running_sums(decay_rows):
    total = decay_rows
    place = lax.broadcasted_iota(jnp.int32, total.shape, 1)
    reach = 1
    while reach < total.shape[1]:
        total = total + jnp.where(place >= reach, pltpu.roll(total, reach, 1), 0.0)
        reach *= 2
    return total


def turned(rows):
    fill = jnp.zeros((HD - rows.shape[0], rows.shape[1]), rows.dtype)
    return jnp.transpose(jnp.concatenate([rows, fill], axis=0))


def states_kernel(key_ref, value_ref, decay_ref, *state_refs):
    running = running_sums(decay_ref[0])
    press = turned(jnp.exp(running[:, BLK - 1 :] - running))
    states = []
    for h in range(running.shape[0]):
        lanes = slice(h * HD, (h + 1) * HD)
        pressed = (key_ref[0, :, lanes].astype(jnp.float32) * press[:, h : h + 1]).astype(jnp.bfloat16)
        states.append(
            lax.dot_general(
                pressed, value_ref[0, :, lanes], (((0,), (0,)), ((), ())), preferred_element_type=jnp.float32
            )
        )
    for part, state_ref in enumerate(state_refs):

        @pl.when(pl.program_id(0) == part)
        def _(state_ref=state_ref):
            for h, state in enumerate(states):
                state_ref[h] = state.astype(state_ref.dtype)


def closing_states(lin_key, lin_value, decay_rows, parts):
    heads = decay_rows.shape[1] // parts
    wide = pl.BlockSpec((1, BLK, heads * HD), lambda i: (0, 0, i))
    return pl.pallas_call(
        states_kernel,
        grid=(parts,),
        in_specs=[wide, wide, pl.BlockSpec((1, heads, BLK), lambda i: (0, i, 0))],
        out_specs=[pl.BlockSpec((heads, HD, HD), lambda i: (0, 0, 0))] * parts,
        out_shape=[jax.ShapeDtypeStruct((heads, HD, HD), jnp.bfloat16)] * parts,
        compiler_params=pltpu.CompilerParams(vmem_limit_bytes=16 * MIB),
        name="closing_states",
    )(lin_key, lin_value, decay_rows)


def mix_kernel(place_ref, query_ref, key_ref, value_ref, decay_ref, gate_ref, gain_ref, state_ref, *out_refs):
    running = running_sums(decay_ref[0])
    columns = turned(running)
    lift = jnp.exp(columns)
    causal = lax.broadcasted_iota(jnp.int32, (HALF, HALF), 0) >= lax.broadcasted_iota(
        jnp.int32, (HALF, HALF), 1
    )
    turned_dims = (((1,), (1,)), ((), ()))
    owner = []
    for out_ref in out_refs:
        first = len(owner)
        owner += [(out_ref, first)] * (out_ref.shape[2] // HD)
    for h in range(state_ref.shape[0]):
        lanes = slice(h * HD, (h + 1) * HD)
        queries = query_ref[0, :, lanes]
        keys = key_ref[0, :, lanes]
        values = value_ref[0, :, lanes]
        column = columns[:, h : h + 1]
        row = running[h : h + 1, :]
        earlier = jnp.dot(queries, state_ref[h], preferred_element_type=jnp.float32) * lift[:, h : h + 1]
        earlier = jnp.where(place_ref[0] > 0, earlier, 0.0)
        parts = []
        for b in range(2):
            rows = slice(b * HALF, (b + 1) * HALF)
            seen = (b + 1) * HALF
            scores = lax.dot_general(
                queries[rows], keys[:seen], turned_dims, preferred_element_type=jnp.float32
            )
            pieces = []
            for c in range(b + 1):
                span = slice(c * HALF, (c + 1) * HALF)
                gap = column[rows] - row[:, span]
                if c == b:
                    fall = jnp.where(causal, jnp.exp(jnp.where(causal, gap, 0.0)), 0.0)
                else:
                    fall = jnp.exp(gap)
                pieces.append((scores[:, span] * fall).astype(jnp.bfloat16))
            weights = pieces[0] if b == 0 else jnp.concatenate(pieces, axis=1)
            parts.append(jnp.dot(weights, values[:seen], preferred_element_type=jnp.float32))
        mixture = jnp.concatenate(parts, axis=0) + earlier
        scale = lax.rsqrt(jnp.mean(mixture * mixture, axis=1, keepdims=True) + epsilon)
        gate = jax.nn.sigmoid(gate_ref[0, :, lanes].astype(jnp.float32))
        result = mixture * scale * gain_ref[0:1, lanes] * gate
        out_ref, first = owner[h]
        lanes = slice((h - first) * HD, (h - first + 1) * HD)
        out_ref[0, :, lanes] = result.astype(out_ref.dtype)


def lightning(
    place, lin_query, lin_key, lin_value, decay_rows, out_gate, norm_gain, incoming, part, parts, chunks
):
    heads = decay_rows.shape[1] // parts
    wide = pl.BlockSpec((1, BLK, heads * HD), lambda i, place: (0, 0, part))
    return pl.pallas_call(
        mix_kernel,
        grid_spec=pltpu.PrefetchScalarGridSpec(
            num_scalar_prefetch=1,
            grid=(1,),
            in_specs=[
                wide,
                wide,
                wide,
                pl.BlockSpec((1, heads, BLK), lambda i, place: (0, part, 0)),
                wide,
                pl.BlockSpec((1, heads * HD), lambda i, place: (0, part)),
                pl.BlockSpec((heads, HD, HD), lambda i, place: (0, 0, 0)),
            ],
            out_specs=[pl.BlockSpec((1, BLK, n * HD), lambda i, place: (0, 0, 0)) for n in chunks],
        ),
        out_shape=[jax.ShapeDtypeStruct((1, BLK, n * HD), jnp.bfloat16) for n in chunks],
        compiler_params=pltpu.CompilerParams(vmem_limit_bytes=20 * MIB),
        name="lightning_mix",
    )(place, lin_query, lin_key, lin_value, decay_rows, out_gate, norm_gain, incoming)


def copied(pieces, sems):
    copies = [pltpu.make_async_copy(a, b, sems.at[i]) for i, (a, b) in enumerate(pieces)]
    for copy in copies:
        copy.start()
    for copy in copies:
        copy.wait()


def pack_kernel(query_ref, key_ref, value_ref, raw_ref, *refs):
    width = GROUP * HD
    pieces = [
        (query_ref.at[:, :, pl.ds(0, width)], raw_ref.at[:, :, pl.ds(0, width)]),
        (key_ref.at[:, :, pl.ds(0, HD)], raw_ref.at[:, :, pl.ds(width, HD)]),
        (value_ref.at[:, :, pl.ds(0, HD)], raw_ref.at[:, :, pl.ds(width + HD, HD)]),
    ]
    for i, pair_ref in enumerate(refs[:-1]):
        lanes = pl.ds((i + 1) * HD, HD)
        pieces.append((key_ref.at[:, :, lanes], pair_ref.at[:, :, pl.ds(0, HD)]))
        pieces.append((value_ref.at[:, :, lanes], pair_ref.at[:, :, pl.ds(HD, HD)]))
    copied(pieces, refs[-1])


def packed(soft_query, soft_key, soft_value):
    kv_count = soft_key.shape[2] // HD
    widths = [(GROUP + 2) * HD] + [2 * HD] * (kv_count - 1)
    return pl.pallas_call(
        pack_kernel,
        in_specs=[pl.BlockSpec(memory_space=pltpu.HBM)] * 3,
        out_specs=[pl.BlockSpec(memory_space=pltpu.VMEM)] * kv_count,
        out_shape=[pltpu.VMEM((1, BLK, width), jnp.bfloat16) for width in widths],
        scratch_shapes=[pltpu.SemaphoreType.DMA((1 + 2 * kv_count,))],
        compiler_params=pltpu.CompilerParams(vmem_limit_bytes=4 * MIB),
        name="packed",
    )(soft_query, soft_key, soft_value)


def attend(place, query_ref, key_ref, value_ref, before_ref, out_ref):
    others = before_ref.shape[0]
    factor = HD ** (-0.5) * LOG2E
    causal = lax.broadcasted_iota(jnp.int32, (BLK, BLK), 0) >= lax.broadcasted_iota(jnp.int32, (BLK, BLK), 1)
    turned_dims = (((1,), (1,)), ((), ()))
    keys, values = slice(0, HD), slice(HD, 2 * HD)

    def scored(queries, keys):
        return lax.dot_general(queries, keys, turned_dims, preferred_element_type=jnp.float32)

    for h in range(query_ref.shape[2] // HD):
        lanes = slice(h * HD, (h + 1) * HD)
        queries = query_ref[0, :, lanes]
        own = jnp.where(causal, scored(queries, key_ref[0]), lowest)
        peak = jnp.max(own, axis=1, keepdims=True)
        if others == 1:
            before = jnp.where(place > 0, scored(queries, before_ref[0, :, keys]), lowest)
            peak = jnp.maximum(peak, jnp.max(before, axis=1, keepdims=True))
            own = jnp.exp2((own - peak) * factor)
            before = jnp.exp2((before - peak) * factor)
            totals = jnp.sum(own, axis=1, keepdims=True) + jnp.sum(before, axis=1, keepdims=True)
            weighted = jnp.dot(
                own.astype(jnp.bfloat16), value_ref[0], preferred_element_type=jnp.float32
            ) + jnp.dot(
                before.astype(jnp.bfloat16), before_ref[0, :, values], preferred_element_type=jnp.float32
            )
        else:
            own = jnp.exp2((own - peak) * factor)
            totals = jnp.sum(own, axis=1, keepdims=True)
            weighted = jnp.dot(
                own.astype(jnp.bfloat16), value_ref[0], preferred_element_type=jnp.float32
            )

            def absorb(turn, kept):
                peak, totals, weighted = kept
                scores = scored(queries, before_ref[turn, :, keys])
                new_peak = jnp.maximum(peak, jnp.max(scores, axis=1, keepdims=True))
                shrink = jnp.exp2((peak - new_peak) * factor)
                scores = jnp.exp2((scores - new_peak) * factor)
                totals = totals * shrink + jnp.sum(scores, axis=1, keepdims=True)
                weighted = weighted * shrink + jnp.dot(
                    scores.astype(jnp.bfloat16),
                    before_ref[turn, :, values],
                    preferred_element_type=jnp.float32,
                )
                return (new_peak, totals, weighted)

            peak, totals, weighted = lax.fori_loop(0, place, absorb, (peak, totals, weighted))
        out_ref[0, :, lanes] = (weighted / totals).astype(out_ref.dtype)


def soft_kernel(place_ref, query_ref, key_ref, value_ref, before_ref, out_ref):
    attend(place_ref[0], query_ref, key_ref, value_ref, before_ref, out_ref)


STEP = 8


def softmax_group(place, soft_query, pair, before, group):
    others = before.shape[0]
    steps = GROUP // STEP
    wide = (1, BLK, STEP * HD)
    return pl.pallas_call(
        soft_kernel,
        grid_spec=pltpu.PrefetchScalarGridSpec(
            num_scalar_prefetch=1,
            grid=(steps,),
            in_specs=[
                pl.BlockSpec(wide, lambda i, place: (0, 0, group * steps + i)),
                pl.BlockSpec((1, BLK, HD), lambda i, place: (0, 0, 0)),
                pl.BlockSpec((1, BLK, HD), lambda i, place: (0, 0, 1)),
                pl.BlockSpec((others, BLK, 2 * HD), lambda i, place: (0, 0, 0)),
            ],
            out_specs=pl.BlockSpec(wide, lambda i, place: (0, 0, i)),
        ),
        out_shape=jax.ShapeDtypeStruct((1, BLK, GROUP * HD), jnp.bfloat16),
        compiler_params=pltpu.CompilerParams(vmem_limit_bytes=20 * MIB),
        name="softmax_group",
    )(place, soft_query, pair, pair, before)


def finish_kernel(place_ref, query_ref, key_ref, value_ref, before_ref, ready_ref, out_ref):
    here = pl.program_id(0) < GROUP // STEP

    @pl.when(here)
    def _():
        attend(place_ref[0], query_ref, key_ref, value_ref, before_ref, out_ref)

    @pl.when(jnp.logical_not(here))
    def _():
        out_ref[...] = ready_ref[...]


def softmax_finish(place, raw, before, ready):
    others = before.shape[0]
    steps = GROUP // STEP
    wide = (1, BLK, STEP * HD)
    groups = 1 + ready.shape[2] // (GROUP * HD)
    return pl.pallas_call(
        finish_kernel,
        grid_spec=pltpu.PrefetchScalarGridSpec(
            num_scalar_prefetch=1,
            grid=(groups * steps,),
            in_specs=[
                pl.BlockSpec(wide, lambda i, place: (0, 0, jnp.minimum(i, steps - 1))),
                pl.BlockSpec((1, BLK, HD), lambda i, place: (0, 0, GROUP)),
                pl.BlockSpec((1, BLK, HD), lambda i, place: (0, 0, GROUP + 1)),
                pl.BlockSpec((others, BLK, 2 * HD), lambda i, place: (0, 0, 0)),
                pl.BlockSpec(wide, lambda i, place: (0, 0, jnp.maximum(i - steps, 0))),
            ],
            out_specs=pl.BlockSpec(wide, lambda i, place: (0, 0, i)),
        ),
        out_shape=jax.ShapeDtypeStruct((1, BLK, groups * GROUP * HD), jnp.bfloat16),
        compiler_params=pltpu.CompilerParams(vmem_limit_bytes=20 * MIB),
        name="softmax_finish",
    )(place, raw, raw, raw, before, ready)


def place_kernel(start, block_ref, *refs):
    whole_ref, sems = refs[-2:]
    copied([(block_ref, whole_ref.at[:, :, pl.ds(start, block_ref.shape[2])])], sems)


def placed(block, start, width, whole=None):
    anywhere = pl.BlockSpec(memory_space=pl.ANY)
    operands = (block,) if whole is None else (block, whole)
    return pl.pallas_call(
        functools.partial(place_kernel, start),
        in_specs=[anywhere] * len(operands),
        out_specs=anywhere,
        out_shape=jax.ShapeDtypeStruct(block.shape[:2] + (width,), block.dtype),
        scratch_shapes=[pltpu.SemaphoreType.DMA((1,))],
        input_output_aliases={} if whole is None else {1: 0},
        compiler_params=pltpu.CompilerParams(vmem_limit_bytes=1 * MIB),
        name="placed",
    )(*operands)


def earlier_blocks(block):
    devices = lax.axis_size("ctx")
    if devices == 2:
        return passed_along(block, "ctx", 1)
    return lax.all_gather(block, "ctx", axis=0, tiled=True)[: devices - 1]


def incoming_states(closing, decay_rows):
    if lax.axis_size("ctx") == 2:
        return passed_along(closing, "ctx", 1)
    states = lax.all_gather(closing[None], "ctx", axis=0, tiled=True)
    logs = lax.all_gather(jnp.sum(decay_rows, axis=2), "ctx", axis=0, tiled=True)
    earlier = (lax.iota(jnp.int32, logs.shape[0]) < lax.axis_index("ctx"))[:, None]
    reached = jnp.sum(jnp.where(earlier, logs, 0.0), axis=0)
    rising = jnp.cumsum(logs, axis=0)
    weight = jnp.where(earlier, jnp.exp(jnp.where(earlier, reached[None, :] - rising, 0.0)), 0.0)
    return jnp.sum(weight[:, :, None, None] * states.astype(jnp.float32), axis=0).astype(jnp.bfloat16)


PARTS = 2
LAST = 2


def local(
    lin_query, lin_key, lin_value, log_decay, out_gate, norm_gain, soft_query, soft_key, soft_value
):
    place = lax.axis_index("ctx").astype(jnp.int32)[None]
    lin_query, lin_key, lin_value, out_gate, soft_query, soft_key, soft_value = (
        pltpu.with_memory_space_constraint(x, pltpu.HBM)
        for x in (lin_query, lin_key, lin_value, out_gate, soft_query, soft_key, soft_value)
    )
    decay_rows = jnp.swapaxes(log_decay, 1, 2)
    heads = decay_rows.shape[1] // PARTS
    raw, *pairs = packed(soft_query, soft_key, soft_value)
    handed_raw = passed_along(raw, "pp", 1)
    befores = [earlier_blocks(pair) for pair in pairs]
    lin_key, lin_value, raw = lax.optimization_barrier((lin_key, lin_value, raw))
    closing = list(closing_states(lin_key, lin_value, decay_rows, PARTS))
    closing[0], *befores = lax.optimization_barrier((closing[0], *befores))
    ready = [
        softmax_group(place, soft_query, pair, before, g + 1)
        for g, (pair, before) in enumerate(zip(pairs, befores))
    ]
    incoming = [
        incoming_states(closing[part], decay_rows[:, part * heads : (part + 1) * heads])
        for part in range(PARTS)
    ]
    ready = [passed_along(group, "pp", 1) for group in ready]
    ready = ready[0] if len(ready) == 1 else jnp.concatenate(ready, axis=2)
    incoming[0], handed_raw = lax.optimization_barrier((incoming[0], handed_raw))
    chunks = []
    for part in range(PARTS):
        chunks += lightning(
            place,
            lin_query,
            lin_key,
            lin_value,
            decay_rows,
            out_gate,
            norm_gain,
            incoming[part],
            part,
            PARTS,
            [heads - LAST, LAST] if part == PARTS - 1 else [heads],
        )
    chunks = [passed_along(chunk, "pp", 1) for chunk in chunks]
    before = earlier_blocks(handed_raw[:, :, GROUP * HD :])
    soft_handed = softmax_finish(place, handed_raw, before, ready)
    lin_handed = None
    start = 0
    for chunk in chunks:
        lin_handed = placed(chunk, start, lin_query.shape[2], lin_handed)
        start += chunk.shape[2]
    return (lin_handed, soft_handed)


def solution(mesh):
    wide = P("pp", "ctx", "tp")
    return jax.shard_map(
        local,
        mesh=mesh,
        in_specs=(wide, wide, wide, wide, wide, P("pp", "tp"), wide, wide, wide),
        out_specs=(wide, wide),
        check_vma=False,
    )
```

```python
import functools

import jax
import jax.numpy as jnp
from jax import lax
from jax.experimental import pallas as pl
from jax.experimental.pallas import tpu as pltpu
from jax.sharding import PartitionSpec as P

HEADS = 64
KV_HEADS = 8
HD = 128
BLK = 256
GROUP = HEADS // KV_HEADS
HALF = BLK // 2

epsilon = 1e-06
lowest = -1e30
LOG2E = 1.4426950408889634
MIB = 1 << 20


def passed_along(block, axis, distance):
    devices = lax.axis_size(axis)
    return lax.ppermute(block, axis, [((i - distance) % devices, i) for i in range(devices)])


def running_sums(decay_rows):
    total = decay_rows
    place = lax.broadcasted_iota(jnp.int32, total.shape, 1)
    reach = 1
    while reach < total.shape[1]:
        total = total + jnp.where(place >= reach, pltpu.roll(total, reach, 1), 0.0)
        reach *= 2
    return total


def turned(rows):
    fill = jnp.zeros((HD - rows.shape[0], rows.shape[1]), rows.dtype)
    return jnp.transpose(jnp.concatenate([rows, fill], axis=0))


def states_kernel(key_ref, value_ref, decay_ref, *state_refs):
    running = running_sums(decay_ref[0])
    press = turned(jnp.exp(running[:, BLK - 1 :] - running))
    states = []
    for h in range(running.shape[0]):
        lanes = slice(h * HD, (h + 1) * HD)
        pressed = (key_ref[0, :, lanes].astype(jnp.float32) * press[:, h : h + 1]).astype(jnp.bfloat16)
        states.append(
            lax.dot_general(
                pressed, value_ref[0, :, lanes], (((0,), (0,)), ((), ())), preferred_element_type=jnp.float32
            )
        )
    for part, state_ref in enumerate(state_refs):

        @pl.when(pl.program_id(0) == part)
        def _(state_ref=state_ref):
            for h, state in enumerate(states):
                state_ref[h] = state.astype(state_ref.dtype)


def closing_states(lin_key, lin_value, decay_rows, parts):
    heads = decay_rows.shape[1] // parts
    wide = pl.BlockSpec((1, BLK, heads * HD), lambda i: (0, 0, i))
    return pl.pallas_call(
        states_kernel,
        grid=(parts,),
        in_specs=[wide, wide, pl.BlockSpec((1, heads, BLK), lambda i: (0, i, 0))],
        out_specs=[pl.BlockSpec((heads, HD, HD), lambda i: (0, 0, 0))] * parts,
        out_shape=[jax.ShapeDtypeStruct((heads, HD, HD), jnp.bfloat16)] * parts,
        compiler_params=pltpu.CompilerParams(vmem_limit_bytes=16 * MIB),
        name="closing_states",
    )(lin_key, lin_value, decay_rows)


def mix_kernel(place_ref, query_ref, key_ref, value_ref, decay_ref, gate_ref, gain_ref, state_ref, *out_refs):
    running = running_sums(decay_ref[0])
    columns = turned(running)
    lift = jnp.exp(columns)
    causal = lax.broadcasted_iota(jnp.int32, (HALF, HALF), 0) >= lax.broadcasted_iota(
        jnp.int32, (HALF, HALF), 1
    )
    turned_dims = (((1,), (1,)), ((), ()))
    owner = []
    for out_ref in out_refs:
        first = len(owner)
        owner += [(out_ref, first)] * (out_ref.shape[2] // HD)
    for h in range(state_ref.shape[0]):
        lanes = slice(h * HD, (h + 1) * HD)
        queries = query_ref[0, :, lanes]
        keys = key_ref[0, :, lanes]
        values = value_ref[0, :, lanes]
        column = columns[:, h : h + 1]
        row = running[h : h + 1, :]
        earlier = jnp.dot(queries, state_ref[h], preferred_element_type=jnp.float32) * lift[:, h : h + 1]
        earlier = jnp.where(place_ref[0] > 0, earlier, 0.0)
        parts = []
        for b in range(2):
            rows = slice(b * HALF, (b + 1) * HALF)
            seen = (b + 1) * HALF
            scores = lax.dot_general(
                queries[rows], keys[:seen], turned_dims, preferred_element_type=jnp.float32
            )
            pieces = []
            for c in range(b + 1):
                span = slice(c * HALF, (c + 1) * HALF)
                gap = column[rows] - row[:, span]
                if c == b:
                    fall = jnp.where(causal, jnp.exp(jnp.where(causal, gap, 0.0)), 0.0)
                else:
                    fall = jnp.exp(gap)
                pieces.append((scores[:, span] * fall).astype(jnp.bfloat16))
            weights = pieces[0] if b == 0 else jnp.concatenate(pieces, axis=1)
            parts.append(jnp.dot(weights, values[:seen], preferred_element_type=jnp.float32))
        mixture = jnp.concatenate(parts, axis=0) + earlier
        scale = lax.rsqrt(jnp.mean(mixture * mixture, axis=1, keepdims=True) + epsilon)
        gate = jax.nn.sigmoid(gate_ref[0, :, lanes].astype(jnp.float32))
        result = mixture * scale * gain_ref[0:1, lanes] * gate
        out_ref, first = owner[h]
        lanes = slice((h - first) * HD, (h - first + 1) * HD)
        out_ref[0, :, lanes] = result.astype(out_ref.dtype)


def lightning(
    place, lin_query, lin_key, lin_value, decay_rows, out_gate, norm_gain, incoming, part, parts, chunks
):
    heads = decay_rows.shape[1] // parts
    wide = pl.BlockSpec((1, BLK, heads * HD), lambda i, place: (0, 0, part))
    return pl.pallas_call(
        mix_kernel,
        grid_spec=pltpu.PrefetchScalarGridSpec(
            num_scalar_prefetch=1,
            grid=(1,),
            in_specs=[
                wide,
                wide,
                wide,
                pl.BlockSpec((1, heads, BLK), lambda i, place: (0, part, 0)),
                wide,
                pl.BlockSpec((1, heads * HD), lambda i, place: (0, part)),
                pl.BlockSpec((heads, HD, HD), lambda i, place: (0, 0, 0)),
            ],
            out_specs=[pl.BlockSpec((1, BLK, n * HD), lambda i, place: (0, 0, 0)) for n in chunks],
        ),
        out_shape=[jax.ShapeDtypeStruct((1, BLK, n * HD), jnp.bfloat16) for n in chunks],
        compiler_params=pltpu.CompilerParams(vmem_limit_bytes=20 * MIB),
        name="lightning_mix",
    )(place, lin_query, lin_key, lin_value, decay_rows, out_gate, norm_gain, incoming)


def copied(pieces, sems):
    copies = [pltpu.make_async_copy(a, b, sems.at[i]) for i, (a, b) in enumerate(pieces)]
    for copy in copies:
        copy.start()
    for copy in copies:
        copy.wait()


def pack_kernel(query_ref, key_ref, value_ref, raw_ref, *refs):
    width = GROUP * HD
    pieces = [
        (query_ref.at[:, :, pl.ds(0, width)], raw_ref.at[:, :, pl.ds(0, width)]),
        (key_ref.at[:, :, pl.ds(0, HD)], raw_ref.at[:, :, pl.ds(width, HD)]),
        (value_ref.at[:, :, pl.ds(0, HD)], raw_ref.at[:, :, pl.ds(width + HD, HD)]),
    ]
    for i, pair_ref in enumerate(refs[:-1]):
        lanes = pl.ds((i + 1) * HD, HD)
        pieces.append((key_ref.at[:, :, lanes], pair_ref.at[:, :, pl.ds(0, HD)]))
        pieces.append((value_ref.at[:, :, lanes], pair_ref.at[:, :, pl.ds(HD, HD)]))
    copied(pieces, refs[-1])


def packed(soft_query, soft_key, soft_value):
    kv_count = soft_key.shape[2] // HD
    widths = [(GROUP + 2) * HD] + [2 * HD] * (kv_count - 1)
    return pl.pallas_call(
        pack_kernel,
        in_specs=[pl.BlockSpec(memory_space=pltpu.HBM)] * 3,
        out_specs=[pl.BlockSpec(memory_space=pltpu.VMEM)] * kv_count,
        out_shape=[pltpu.VMEM((1, BLK, width), jnp.bfloat16) for width in widths],
        scratch_shapes=[pltpu.SemaphoreType.DMA((1 + 2 * kv_count,))],
        compiler_params=pltpu.CompilerParams(vmem_limit_bytes=4 * MIB),
        name="packed",
    )(soft_query, soft_key, soft_value)


def attend(place, query_ref, key_ref, value_ref, before_key_ref, before_value_ref, out_ref):
    others = before_key_ref.shape[0]
    factor = HD ** (-0.5) * LOG2E
    causal = lax.broadcasted_iota(jnp.int32, (BLK, BLK), 0) >= lax.broadcasted_iota(jnp.int32, (BLK, BLK), 1)
    turned_dims = (((1,), (1,)), ((), ()))

    def scored(queries, keys):
        return lax.dot_general(queries, keys, turned_dims, preferred_element_type=jnp.float32)

    for h in range(query_ref.shape[2] // HD):
        lanes = slice(h * HD, (h + 1) * HD)
        queries = query_ref[0, :, lanes]
        own = jnp.where(causal, scored(queries, key_ref[0]), lowest)
        peak = jnp.max(own, axis=1, keepdims=True)
        if others == 1:
            before = jnp.where(place > 0, scored(queries, before_key_ref[0]), lowest)
            peak = jnp.maximum(peak, jnp.max(before, axis=1, keepdims=True))
            own = jnp.exp2((own - peak) * factor)
            before = jnp.exp2((before - peak) * factor)
            totals = jnp.sum(own, axis=1, keepdims=True) + jnp.sum(before, axis=1, keepdims=True)
            weighted = jnp.dot(
                own.astype(jnp.bfloat16), value_ref[0], preferred_element_type=jnp.float32
            ) + jnp.dot(
                before.astype(jnp.bfloat16), before_value_ref[0], preferred_element_type=jnp.float32
            )
        else:
            own = jnp.exp2((own - peak) * factor)
            totals = jnp.sum(own, axis=1, keepdims=True)
            weighted = jnp.dot(
                own.astype(jnp.bfloat16), value_ref[0], preferred_element_type=jnp.float32
            )

            def absorb(turn, kept):
                peak, totals, weighted = kept
                scores = scored(queries, before_key_ref[turn])
                new_peak = jnp.maximum(peak, jnp.max(scores, axis=1, keepdims=True))
                shrink = jnp.exp2((peak - new_peak) * factor)
                scores = jnp.exp2((scores - new_peak) * factor)
                totals = totals * shrink + jnp.sum(scores, axis=1, keepdims=True)
                weighted = weighted * shrink + jnp.dot(
                    scores.astype(jnp.bfloat16),
                    before_value_ref[turn],
                    preferred_element_type=jnp.float32,
                )
                return (new_peak, totals, weighted)

            peak, totals, weighted = lax.fori_loop(0, place, absorb, (peak, totals, weighted))
        out_ref[0, :, lanes] = (weighted / totals).astype(out_ref.dtype)


def soft_kernel(place_ref, query_ref, key_ref, value_ref, before_key_ref, before_value_ref, out_ref):
    attend(place_ref[0], query_ref, key_ref, value_ref, before_key_ref, before_value_ref, out_ref)


def lanes_at(rows, width, index):
    return pl.BlockSpec((rows, BLK, width), lambda i, place: (0, 0, index))


def softmax_heads(place, soft_query, first, count, key, value, before_key, before_value):
    others = before_key[0].shape[0]
    return pl.pallas_call(
        soft_kernel,
        grid_spec=pltpu.PrefetchScalarGridSpec(
            num_scalar_prefetch=1,
            grid=(1,),
            in_specs=[
                lanes_at(1, count * HD, first // count),
                lanes_at(1, HD, key[1]),
                lanes_at(1, HD, value[1]),
                lanes_at(others, HD, before_key[1]),
                lanes_at(others, HD, before_value[1]),
            ],
            out_specs=lanes_at(1, count * HD, 0),
        ),
        out_shape=jax.ShapeDtypeStruct((1, BLK, count * HD), jnp.bfloat16),
        compiler_params=pltpu.CompilerParams(vmem_limit_bytes=20 * MIB),
        name="softmax_heads",
    )(place, soft_query, key[0], value[0], before_key[0], before_value[0])


def softmax_all(place, query, key, value, before_key, before_value):
    groups = key.shape[2] // HD
    others = before_key.shape[0]

    def by_group(rows, width):
        return pl.BlockSpec((rows, BLK, width), lambda i, place: (0, 0, i))

    return pl.pallas_call(
        soft_kernel,
        grid_spec=pltpu.PrefetchScalarGridSpec(
            num_scalar_prefetch=1,
            grid=(groups,),
            in_specs=[
                by_group(1, GROUP * HD),
                by_group(1, HD),
                by_group(1, HD),
                by_group(others, HD),
                by_group(others, HD),
            ],
            out_specs=by_group(1, GROUP * HD),
        ),
        out_shape=pltpu.HBM(query.shape, jnp.bfloat16),
        compiler_params=pltpu.CompilerParams(vmem_limit_bytes=20 * MIB),
        name="softmax_all",
    )(place, query, key, value, before_key, before_value)


def finish_kernel(
    place_ref, query_ref, key_ref, value_ref, before_key_ref, before_value_ref, ready_ref, out_ref
):
    here = pl.program_id(0) == 0

    @pl.when(here)
    def _():
        attend(place_ref[0], query_ref, key_ref, value_ref, before_key_ref, before_value_ref, out_ref)

    @pl.when(jnp.logical_not(here))
    def _():
        out_ref[...] = ready_ref[...]


def softmax_finish(place, raw, before, ready):
    others = before.shape[0]
    width = GROUP * HD
    groups = 1 + ready.shape[2] // width
    return pl.pallas_call(
        finish_kernel,
        grid_spec=pltpu.PrefetchScalarGridSpec(
            num_scalar_prefetch=1,
            grid=(groups,),
            in_specs=[
                lanes_at(1, width, 0),
                lanes_at(1, HD, GROUP),
                lanes_at(1, HD, GROUP + 1),
                lanes_at(others, HD, 0),
                lanes_at(others, HD, 1),
                pl.BlockSpec((1, BLK, width), lambda i, place: (0, 0, jnp.maximum(i - 1, 0))),
            ],
            out_specs=pl.BlockSpec((1, BLK, width), lambda i, place: (0, 0, i)),
        ),
        out_shape=pltpu.HBM((1, BLK, groups * width), jnp.bfloat16),
        compiler_params=pltpu.CompilerParams(vmem_limit_bytes=20 * MIB),
        name="softmax_finish",
    )(place, raw, raw, raw, before, before, ready)


def place_kernel(start, block_ref, *refs):
    whole_ref, sems = refs[-2:]
    copied([(block_ref, whole_ref.at[:, :, pl.ds(start, block_ref.shape[2])])], sems)


def placed(block, start, width, whole=None):
    anywhere = pl.BlockSpec(memory_space=pl.ANY)
    in_hbm = pl.BlockSpec(memory_space=pltpu.HBM)
    operands = (block,) if whole is None else (block, whole)
    return pl.pallas_call(
        functools.partial(place_kernel, start),
        in_specs=[anywhere] + [in_hbm] * (len(operands) - 1),
        out_specs=in_hbm,
        out_shape=pltpu.HBM(block.shape[:2] + (width,), block.dtype),
        scratch_shapes=[pltpu.SemaphoreType.DMA((1,))],
        input_output_aliases={} if whole is None else {1: 0},
        compiler_params=pltpu.CompilerParams(vmem_limit_bytes=1 * MIB),
        name="placed",
    )(*operands)


def earlier_blocks(block):
    devices = lax.axis_size("ctx")
    if devices == 2:
        return passed_along(block, "ctx", 1)
    return lax.all_gather(block, "ctx", axis=0, tiled=True)[: devices - 1]


def incoming_states(closing, device_log):
    if lax.axis_size("ctx") == 2:
        return passed_along(closing, "ctx", 1)
    states = lax.all_gather(closing[None], "ctx", axis=0, tiled=True)
    logs = lax.all_gather(device_log, "ctx", axis=0, tiled=True)
    earlier = (lax.iota(jnp.int32, logs.shape[0]) < lax.axis_index("ctx"))[:, None]
    reached = jnp.sum(jnp.where(earlier, logs, 0.0), axis=0)
    rising = jnp.cumsum(logs, axis=0)
    weight = jnp.where(earlier, jnp.exp(jnp.where(earlier, reached[None, :] - rising, 0.0)), 0.0)
    return jnp.sum(weight[:, :, None, None] * states.astype(jnp.float32), axis=0).astype(jnp.bfloat16)


PARTS = 2
LAST = 2


def joined(chunks, width):
    whole = None
    start = 0
    for chunk in chunks:
        whole = placed(chunk, start, width, whole)
        start += chunk.shape[2]
    return whole


def lightning_chunks(place, arrays, incoming):
    heads = incoming[0].shape[0]
    chunks = []
    for part in range(PARTS):
        sizes = [heads - LAST, LAST] if part == PARTS - 1 else [heads]
        chunks += lightning(place, *arrays, incoming[part], part, PARTS, sizes)
    return [passed_along(chunk, "pp", 1) for chunk in chunks]


def ahead(
    device_logs,
    lin_query,
    lin_key,
    lin_value,
    decay_rows,
    out_gate,
    norm_gain,
    soft_query,
    soft_key,
    soft_value,
    place,
):
    raw, *pairs = packed(soft_query, soft_key, soft_value)
    handed_raw = passed_along(raw, "pp", 1)
    befores = [earlier_blocks(pair) for pair in pairs]
    lin_key, lin_value, raw = lax.optimization_barrier((lin_key, lin_value, raw))
    closing = list(closing_states(lin_key, lin_value, decay_rows, PARTS))
    closing[0], *befores = lax.optimization_barrier((closing[0], *befores))
    ready = [
        softmax_heads(
            place, soft_query, (g + 1) * GROUP, GROUP, (pair, 0), (pair, 1), (before, 0), (before, 1)
        )
        for g, (pair, before) in enumerate(zip(pairs, befores))
    ]
    incoming = [incoming_states(closing[part], device_logs[part]) for part in range(PARTS)]
    ready = [passed_along(group, "pp", 1) for group in ready]
    ready = ready[0] if len(ready) == 1 else jnp.concatenate(ready, axis=2)
    incoming[0], handed_raw = lax.optimization_barrier((incoming[0], handed_raw))
    arrays = (lin_query, lin_key, lin_value, decay_rows, out_gate, norm_gain)
    chunks = lightning_chunks(place, arrays, incoming)
    before = earlier_blocks(handed_raw[:, :, GROUP * HD :])
    soft_handed = softmax_finish(place, handed_raw, before, ready)
    return (joined(chunks, lin_query.shape[2]), soft_handed)


def raw_first(
    device_logs,
    lin_query,
    lin_key,
    lin_value,
    decay_rows,
    out_gate,
    norm_gain,
    soft_query,
    soft_key,
    soft_value,
    place,
):
    handed_key = passed_along(soft_key, "pp", 1)
    handed_value = passed_along(soft_value, "pp", 1)
    handed_query = passed_along(soft_query, "pp", 1)
    closing = closing_states(lin_key, lin_value, decay_rows, PARTS)
    incoming = [incoming_states(closing[part], device_logs[part]) for part in range(PARTS)]
    incoming[-1], handed_query, handed_key, handed_value = lax.optimization_barrier(
        (incoming[-1], handed_query, handed_key, handed_value)
    )
    befores = (earlier_blocks(handed_key), earlier_blocks(handed_value))
    arrays = (lin_query, lin_key, lin_value, decay_rows, out_gate, norm_gain)
    chunks = lightning_chunks(place, arrays, incoming)
    soft_handed = softmax_all(place, handed_query, handed_key, handed_value, *befores)
    return (joined(chunks, lin_query.shape[2]), soft_handed)


def worked_out_first(
    device_logs,
    lin_query,
    lin_key,
    lin_value,
    decay_rows,
    out_gate,
    norm_gain,
    soft_query,
    soft_key,
    soft_value,
    place,
):
    kv_count = soft_key.shape[2] // HD
    befores = (earlier_blocks(soft_key), earlier_blocks(soft_value))
    closing = list(closing_states(lin_key, lin_value, decay_rows, PARTS))
    closing[0], *befores = lax.optimization_barrier((closing[0], *befores))
    incoming = [incoming_states(closing[part], device_logs[part]) for part in range(PARTS)]
    groups = []
    for g in range(kv_count):
        if groups:
            soft_query, groups[-1] = lax.optimization_barrier((soft_query, groups[-1]))
        groups.append(
            softmax_heads(
                place,
                soft_query,
                g * GROUP,
                GROUP,
                (soft_key, g),
                (soft_value, g),
                (befores[0], g),
                (befores[1], g),
            )
        )
    groups = [passed_along(group, "pp", 1) for group in groups]
    for part in range(min(PARTS, kv_count)):
        incoming[part], groups[part] = lax.optimization_barrier((incoming[part], groups[part]))
    arrays = (lin_query, lin_key, lin_value, decay_rows, out_gate, norm_gain)
    chunks = lightning_chunks(place, arrays, incoming)
    soft_handed = joined(groups, soft_query.shape[2])
    return (joined(chunks, lin_query.shape[2]), soft_handed)


def local(
    lin_query, lin_key, lin_value, log_decay, out_gate, norm_gain, soft_query, soft_key, soft_value
):
    arrays = (
        lin_query,
        lin_key,
        lin_value,
        jnp.swapaxes(log_decay, 1, 2),
        out_gate,
        norm_gain,
        soft_query,
        soft_key,
        soft_value,
    )
    arrays = tuple(pltpu.with_memory_space_constraint(x, pltpu.HBM) for x in arrays)
    place = lax.axis_index("ctx").astype(jnp.int32)[None]
    if lax.axis_size("ctx") > 2:
        return ahead(jnp.split(jnp.sum(log_decay, axis=1), PARTS, axis=1), *arrays, place)
    turn = lax.axis_index("tp") & 1
    unused = [None] * PARTS
    return lax.cond(turn == 0, functools.partial(raw_first, unused), functools.partial(worked_out_first, unused), *arrays, place)


def solution(mesh):
    wide = P("pp", "ctx", "tp")
    return jax.shard_map(
        local,
        mesh=mesh,
        in_specs=(wide, wide, wide, wide, wide, P("pp", "tp"), wide, wide, wide),
        out_specs=(wide, wide),
        check_vma=False,
    )
```

```python
import functools

import jax
import jax.numpy as jnp
from jax import lax
from jax.experimental import pallas as pl
from jax.experimental.pallas import tpu as pltpu
from jax.sharding import PartitionSpec as P

HEADS = 64
KV_HEADS = 8
HD = 128
BLK = 256
GROUP = HEADS // KV_HEADS
HALF = BLK // 2

epsilon = 1e-06
lowest = -1e30
LOG2E = 1.4426950408889634
MIB = 1 << 20


def passed_along(block, axis, distance):
    devices = lax.axis_size(axis)
    return lax.ppermute(block, axis, [((i - distance) % devices, i) for i in range(devices)])


def running_sums(decay_rows):
    total = decay_rows
    place = lax.broadcasted_iota(jnp.int32, total.shape, 1)
    reach = 1
    while reach < total.shape[1]:
        total = total + jnp.where(place >= reach, pltpu.roll(total, reach, 1), 0.0)
        reach *= 2
    return total


def turned(rows):
    fill = jnp.zeros((HD - rows.shape[0], rows.shape[1]), rows.dtype)
    return jnp.transpose(jnp.concatenate([rows, fill], axis=0))


def states_kernel(key_ref, value_ref, decay_ref, *state_refs):
    running = running_sums(decay_ref[0])
    press = turned(jnp.exp(running[:, BLK - 1 :] - running))
    states = []
    for h in range(running.shape[0]):
        lanes = slice(h * HD, (h + 1) * HD)
        pressed = (key_ref[0, :, lanes].astype(jnp.float32) * press[:, h : h + 1]).astype(jnp.bfloat16)
        states.append(
            lax.dot_general(
                pressed, value_ref[0, :, lanes], (((0,), (0,)), ((), ())), preferred_element_type=jnp.float32
            )
        )
    for part, state_ref in enumerate(state_refs):

        @pl.when(pl.program_id(0) == part)
        def _(state_ref=state_ref):
            for h, state in enumerate(states):
                state_ref[h] = state.astype(state_ref.dtype)


def closing_states(lin_key, lin_value, decay_rows, parts):
    heads = decay_rows.shape[1] // parts
    wide = pl.BlockSpec((1, BLK, heads * HD), lambda i: (0, 0, i))
    return pl.pallas_call(
        states_kernel,
        grid=(parts,),
        in_specs=[wide, wide, pl.BlockSpec((1, heads, BLK), lambda i: (0, i, 0))],
        out_specs=[pl.BlockSpec((heads, HD, HD), lambda i: (0, 0, 0))] * parts,
        out_shape=[jax.ShapeDtypeStruct((heads, HD, HD), jnp.bfloat16)] * parts,
        compiler_params=pltpu.CompilerParams(vmem_limit_bytes=16 * MIB),
        name="closing_states",
    )(lin_key, lin_value, decay_rows)


def mix_kernel(place_ref, query_ref, key_ref, value_ref, decay_ref, gate_ref, gain_ref, state_ref, *out_refs):
    running = running_sums(decay_ref[0])
    columns = turned(running)
    lift = jnp.exp(columns)
    causal = lax.broadcasted_iota(jnp.int32, (HALF, HALF), 0) >= lax.broadcasted_iota(
        jnp.int32, (HALF, HALF), 1
    )
    turned_dims = (((1,), (1,)), ((), ()))
    owner = []
    for out_ref in out_refs:
        first = len(owner)
        owner += [(out_ref, first)] * (out_ref.shape[2] // HD)
    for h in range(state_ref.shape[0]):
        lanes = slice(h * HD, (h + 1) * HD)
        queries = query_ref[0, :, lanes]
        keys = key_ref[0, :, lanes]
        values = value_ref[0, :, lanes]
        column = columns[:, h : h + 1]
        row = running[h : h + 1, :]
        earlier = jnp.dot(queries, state_ref[h], preferred_element_type=jnp.float32) * lift[:, h : h + 1]
        earlier = jnp.where(place_ref[0] > 0, earlier, 0.0)
        parts = []
        for b in range(2):
            rows = slice(b * HALF, (b + 1) * HALF)
            seen = (b + 1) * HALF
            scores = lax.dot_general(
                queries[rows], keys[:seen], turned_dims, preferred_element_type=jnp.float32
            )
            pieces = []
            for c in range(b + 1):
                span = slice(c * HALF, (c + 1) * HALF)
                gap = column[rows] - row[:, span]
                if c == b:
                    fall = jnp.where(causal, jnp.exp(jnp.where(causal, gap, 0.0)), 0.0)
                else:
                    fall = jnp.exp(gap)
                pieces.append((scores[:, span] * fall).astype(jnp.bfloat16))
            weights = pieces[0] if b == 0 else jnp.concatenate(pieces, axis=1)
            parts.append(jnp.dot(weights, values[:seen], preferred_element_type=jnp.float32))
        mixture = jnp.concatenate(parts, axis=0) + earlier
        scale = lax.rsqrt(jnp.mean(mixture * mixture, axis=1, keepdims=True) + epsilon)
        gate = jax.nn.sigmoid(gate_ref[0, :, lanes].astype(jnp.float32))
        result = mixture * scale * gain_ref[0:1, lanes] * gate
        out_ref, first = owner[h]
        lanes = slice((h - first) * HD, (h - first + 1) * HD)
        out_ref[0, :, lanes] = result.astype(out_ref.dtype)


def lightning(
    place, lin_query, lin_key, lin_value, decay_rows, out_gate, norm_gain, incoming, part, parts, chunks
):
    heads = decay_rows.shape[1] // parts
    wide = pl.BlockSpec((1, BLK, heads * HD), lambda i, place: (0, 0, part))
    return pl.pallas_call(
        mix_kernel,
        grid_spec=pltpu.PrefetchScalarGridSpec(
            num_scalar_prefetch=1,
            grid=(1,),
            in_specs=[
                wide,
                wide,
                wide,
                pl.BlockSpec((1, heads, BLK), lambda i, place: (0, part, 0)),
                wide,
                pl.BlockSpec((1, heads * HD), lambda i, place: (0, part)),
                pl.BlockSpec((heads, HD, HD), lambda i, place: (0, 0, 0)),
            ],
            out_specs=[pl.BlockSpec((1, BLK, n * HD), lambda i, place: (0, 0, 0)) for n in chunks],
        ),
        out_shape=[jax.ShapeDtypeStruct((1, BLK, n * HD), jnp.bfloat16) for n in chunks],
        compiler_params=pltpu.CompilerParams(vmem_limit_bytes=20 * MIB),
        name="lightning_mix",
    )(place, lin_query, lin_key, lin_value, decay_rows, out_gate, norm_gain, incoming)


def copied(pieces, sems):
    copies = [pltpu.make_async_copy(a, b, sems.at[i]) for i, (a, b) in enumerate(pieces)]
    for copy in copies:
        copy.start()
    for copy in copies:
        copy.wait()


def pack_kernel(query_ref, key_ref, value_ref, raw_ref, *refs):
    width = GROUP * HD
    pieces = [
        (query_ref.at[:, :, pl.ds(0, width)], raw_ref.at[:, :, pl.ds(0, width)]),
        (key_ref.at[:, :, pl.ds(0, HD)], raw_ref.at[:, :, pl.ds(width, HD)]),
        (value_ref.at[:, :, pl.ds(0, HD)], raw_ref.at[:, :, pl.ds(width + HD, HD)]),
    ]
    for i, pair_ref in enumerate(refs[:-1]):
        lanes = pl.ds((i + 1) * HD, HD)
        pieces.append((key_ref.at[:, :, lanes], pair_ref.at[:, :, pl.ds(0, HD)]))
        pieces.append((value_ref.at[:, :, lanes], pair_ref.at[:, :, pl.ds(HD, HD)]))
    copied(pieces, refs[-1])


def packed(soft_query, soft_key, soft_value):
    kv_count = soft_key.shape[2] // HD
    widths = [(GROUP + 2) * HD] + [2 * HD] * (kv_count - 1)
    return pl.pallas_call(
        pack_kernel,
        in_specs=[pl.BlockSpec(memory_space=pltpu.HBM)] * 3,
        out_specs=[pl.BlockSpec(memory_space=pltpu.VMEM)] * kv_count,
        out_shape=[pltpu.VMEM((1, BLK, width), jnp.bfloat16) for width in widths],
        scratch_shapes=[pltpu.SemaphoreType.DMA((1 + 2 * kv_count,))],
        compiler_params=pltpu.CompilerParams(vmem_limit_bytes=4 * MIB),
        name="packed",
    )(soft_query, soft_key, soft_value)


def attend(place, query_ref, key_ref, value_ref, before_key_ref, before_value_ref, out_ref):
    others = before_key_ref.shape[0]
    factor = HD ** (-0.5) * LOG2E
    causal = lax.broadcasted_iota(jnp.int32, (BLK, BLK), 0) >= lax.broadcasted_iota(jnp.int32, (BLK, BLK), 1)
    turned_dims = (((1,), (1,)), ((), ()))

    def scored(queries, keys):
        return lax.dot_general(queries, keys, turned_dims, preferred_element_type=jnp.float32)

    for h in range(query_ref.shape[2] // HD):
        lanes = slice(h * HD, (h + 1) * HD)
        queries = query_ref[0, :, lanes]
        own = jnp.where(causal, scored(queries, key_ref[0]), lowest)
        peak = jnp.max(own, axis=1, keepdims=True)
        if others == 1:
            before = jnp.where(place > 0, scored(queries, before_key_ref[0]), lowest)
            peak = jnp.maximum(peak, jnp.max(before, axis=1, keepdims=True))
            own = jnp.exp2((own - peak) * factor)
            before = jnp.exp2((before - peak) * factor)
            totals = jnp.sum(own, axis=1, keepdims=True) + jnp.sum(before, axis=1, keepdims=True)
            weighted = jnp.dot(
                own.astype(jnp.bfloat16), value_ref[0], preferred_element_type=jnp.float32
            ) + jnp.dot(
                before.astype(jnp.bfloat16), before_value_ref[0], preferred_element_type=jnp.float32
            )
        else:
            own = jnp.exp2((own - peak) * factor)
            totals = jnp.sum(own, axis=1, keepdims=True)
            weighted = jnp.dot(
                own.astype(jnp.bfloat16), value_ref[0], preferred_element_type=jnp.float32
            )

            def absorb(turn, kept):
                peak, totals, weighted = kept
                scores = scored(queries, before_key_ref[turn])
                new_peak = jnp.maximum(peak, jnp.max(scores, axis=1, keepdims=True))
                shrink = jnp.exp2((peak - new_peak) * factor)
                scores = jnp.exp2((scores - new_peak) * factor)
                totals = totals * shrink + jnp.sum(scores, axis=1, keepdims=True)
                weighted = weighted * shrink + jnp.dot(
                    scores.astype(jnp.bfloat16),
                    before_value_ref[turn],
                    preferred_element_type=jnp.float32,
                )
                return (new_peak, totals, weighted)

            peak, totals, weighted = lax.fori_loop(0, place, absorb, (peak, totals, weighted))
        out_ref[0, :, lanes] = (weighted / totals).astype(out_ref.dtype)


def soft_kernel(place_ref, query_ref, key_ref, value_ref, before_key_ref, before_value_ref, out_ref):
    attend(place_ref[0], query_ref, key_ref, value_ref, before_key_ref, before_value_ref, out_ref)


def lanes_at(rows, width, index):
    return pl.BlockSpec((rows, BLK, width), lambda i, place: (0, 0, index))


def softmax_heads(place, soft_query, first, count, key, value, before_key, before_value):
    others = before_key[0].shape[0]
    return pl.pallas_call(
        soft_kernel,
        grid_spec=pltpu.PrefetchScalarGridSpec(
            num_scalar_prefetch=1,
            grid=(1,),
            in_specs=[
                lanes_at(1, count * HD, first // count),
                lanes_at(1, HD, key[1]),
                lanes_at(1, HD, value[1]),
                lanes_at(others, HD, before_key[1]),
                lanes_at(others, HD, before_value[1]),
            ],
            out_specs=lanes_at(1, count * HD, 0),
        ),
        out_shape=jax.ShapeDtypeStruct((1, BLK, count * HD), jnp.bfloat16),
        compiler_params=pltpu.CompilerParams(vmem_limit_bytes=20 * MIB),
        name="softmax_heads",
    )(place, soft_query, key[0], value[0], before_key[0], before_value[0])


def softmax_all(place, query, pair, before):
    groups = pair.shape[2] // (2 * HD)
    others = before.shape[0]

    def by_group(rows, width, start=0):
        return pl.BlockSpec((rows, BLK, width), lambda i, place: (0, 0, start + i))

    return pl.pallas_call(
        soft_kernel,
        grid_spec=pltpu.PrefetchScalarGridSpec(
            num_scalar_prefetch=1,
            grid=(groups,),
            in_specs=[
                by_group(1, GROUP * HD),
                by_group(1, HD),
                by_group(1, HD, groups),
                by_group(others, HD),
                by_group(others, HD, groups),
            ],
            out_specs=by_group(1, GROUP * HD),
        ),
        out_shape=pltpu.HBM(query.shape, jnp.bfloat16),
        compiler_params=pltpu.CompilerParams(vmem_limit_bytes=20 * MIB),
        name="softmax_all",
    )(place, query, pair, pair, before, before)


def joined_kernel(key_ref, value_ref, out_ref, sems):
    width = key_ref.shape[2]
    copied(
        [
            (key_ref, out_ref.at[:, :, pl.ds(0, width)]),
            (value_ref, out_ref.at[:, :, pl.ds(width, width)]),
        ],
        sems,
    )


def side_by_side(soft_key, soft_value):
    return pl.pallas_call(
        joined_kernel,
        in_specs=[pl.BlockSpec(memory_space=pltpu.HBM)] * 2,
        out_specs=pl.BlockSpec(memory_space=pltpu.VMEM),
        out_shape=pltpu.VMEM((1, BLK, 2 * soft_key.shape[2]), jnp.bfloat16),
        scratch_shapes=[pltpu.SemaphoreType.DMA((2,))],
        compiler_params=pltpu.CompilerParams(vmem_limit_bytes=2 * MIB),
        name="side_by_side",
    )(soft_key, soft_value)


def finish_kernel(
    place_ref, query_ref, key_ref, value_ref, before_key_ref, before_value_ref, ready_ref, out_ref
):
    here = pl.program_id(0) == 0

    @pl.when(here)
    def _():
        attend(place_ref[0], query_ref, key_ref, value_ref, before_key_ref, before_value_ref, out_ref)

    @pl.when(jnp.logical_not(here))
    def _():
        out_ref[...] = ready_ref[...]


def softmax_finish(place, raw, before, ready):
    others = before.shape[0]
    width = GROUP * HD
    groups = 1 + ready.shape[2] // width
    return pl.pallas_call(
        finish_kernel,
        grid_spec=pltpu.PrefetchScalarGridSpec(
            num_scalar_prefetch=1,
            grid=(groups,),
            in_specs=[
                lanes_at(1, width, 0),
                lanes_at(1, HD, GROUP),
                lanes_at(1, HD, GROUP + 1),
                lanes_at(others, HD, 0),
                lanes_at(others, HD, 1),
                pl.BlockSpec((1, BLK, width), lambda i, place: (0, 0, jnp.maximum(i - 1, 0))),
            ],
            out_specs=pl.BlockSpec((1, BLK, width), lambda i, place: (0, 0, i)),
        ),
        out_shape=pltpu.HBM((1, BLK, groups * width), jnp.bfloat16),
        compiler_params=pltpu.CompilerParams(vmem_limit_bytes=20 * MIB),
        name="softmax_finish",
    )(place, raw, raw, raw, before, before, ready)


def place_kernel(start, block_ref, *refs):
    whole_ref, sems = refs[-2:]
    copied([(block_ref, whole_ref.at[:, :, pl.ds(start, block_ref.shape[2])])], sems)


def placed(block, start, width, whole=None):
    anywhere = pl.BlockSpec(memory_space=pl.ANY)
    in_hbm = pl.BlockSpec(memory_space=pltpu.HBM)
    operands = (block,) if whole is None else (block, whole)
    return pl.pallas_call(
        functools.partial(place_kernel, start),
        in_specs=[anywhere] + [in_hbm] * (len(operands) - 1),
        out_specs=in_hbm,
        out_shape=pltpu.HBM(block.shape[:2] + (width,), block.dtype),
        scratch_shapes=[pltpu.SemaphoreType.DMA((1,))],
        input_output_aliases={} if whole is None else {1: 0},
        compiler_params=pltpu.CompilerParams(vmem_limit_bytes=1 * MIB),
        name="placed",
    )(*operands)


def earlier_blocks(block):
    devices = lax.axis_size("ctx")
    if devices == 2:
        return passed_along(block, "ctx", 1)
    return lax.all_gather(block, "ctx", axis=0, tiled=True)[: devices - 1]


def incoming_states(closing, device_log):
    if lax.axis_size("ctx") == 2:
        return passed_along(closing, "ctx", 1)
    states = lax.all_gather(closing[None], "ctx", axis=0, tiled=True)
    logs = lax.all_gather(device_log, "ctx", axis=0, tiled=True)
    earlier = (lax.iota(jnp.int32, logs.shape[0]) < lax.axis_index("ctx"))[:, None]
    reached = jnp.sum(jnp.where(earlier, logs, 0.0), axis=0)
    rising = jnp.cumsum(logs, axis=0)
    weight = jnp.where(earlier, jnp.exp(jnp.where(earlier, reached[None, :] - rising, 0.0)), 0.0)
    return jnp.sum(weight[:, :, None, None] * states.astype(jnp.float32), axis=0).astype(jnp.bfloat16)


PARTS = 2
LAST = 2


def joined(chunks, width):
    whole = None
    start = 0
    for chunk in chunks:
        whole = placed(chunk, start, width, whole)
        start += chunk.shape[2]
    return whole


def lightning_chunks(place, arrays, incoming):
    heads = incoming[0].shape[0]
    chunks = []
    for part in range(PARTS):
        sizes = [heads - LAST, LAST] if part == PARTS - 1 else [heads]
        chunks += lightning(place, *arrays, incoming[part], part, PARTS, sizes)
    return [passed_along(chunk, "pp", 1) for chunk in chunks]


def ahead(
    device_logs,
    lin_query,
    lin_key,
    lin_value,
    decay_rows,
    out_gate,
    norm_gain,
    soft_query,
    soft_key,
    soft_value,
    place,
):
    raw, *pairs = packed(soft_query, soft_key, soft_value)
    handed_raw = passed_along(raw, "pp", 1)
    befores = [earlier_blocks(pair) for pair in pairs]
    lin_key, lin_value, raw = lax.optimization_barrier((lin_key, lin_value, raw))
    closing = list(closing_states(lin_key, lin_value, decay_rows, PARTS))
    closing[0], *befores = lax.optimization_barrier((closing[0], *befores))
    ready = [
        softmax_heads(
            place, soft_query, (g + 1) * GROUP, GROUP, (pair, 0), (pair, 1), (before, 0), (before, 1)
        )
        for g, (pair, before) in enumerate(zip(pairs, befores))
    ]
    incoming = [incoming_states(closing[part], device_logs[part]) for part in range(PARTS)]
    ready = [passed_along(group, "pp", 1) for group in ready]
    ready = ready[0] if len(ready) == 1 else jnp.concatenate(ready, axis=2)
    incoming[0], handed_raw = lax.optimization_barrier((incoming[0], handed_raw))
    arrays = (lin_query, lin_key, lin_value, decay_rows, out_gate, norm_gain)
    chunks = lightning_chunks(place, arrays, incoming)
    before = earlier_blocks(handed_raw[:, :, GROUP * HD :])
    soft_handed = softmax_finish(place, handed_raw, before, ready)
    return (joined(chunks, lin_query.shape[2]), soft_handed)


def raw_first(
    device_logs,
    lin_query,
    lin_key,
    lin_value,
    decay_rows,
    out_gate,
    norm_gain,
    soft_query,
    soft_key,
    soft_value,
    place,
):
    handed_query = passed_along(soft_query, "pp", 1)
    pair = side_by_side(soft_key, soft_value)
    lin_key, lin_value, pair = lax.optimization_barrier((lin_key, lin_value, pair))
    handed_pair = passed_along(pair, "pp", 1)
    closing = closing_states(lin_key, lin_value, decay_rows, PARTS)
    incoming = [incoming_states(closing[part], device_logs[part]) for part in range(PARTS)]
    incoming[-1], handed_query, handed_pair = lax.optimization_barrier((incoming[-1], handed_query, handed_pair))
    arrays = (lin_query, lin_key, lin_value, decay_rows, out_gate, norm_gain)
    chunks = lightning_chunks(place, arrays, incoming)
    soft_handed = softmax_all(place, handed_query, handed_pair, earlier_blocks(handed_pair))
    return (joined(chunks, lin_query.shape[2]), soft_handed)


def worked_out_first(
    device_logs,
    lin_query,
    lin_key,
    lin_value,
    decay_rows,
    out_gate,
    norm_gain,
    soft_query,
    soft_key,
    soft_value,
    place,
):
    kv_count = soft_key.shape[2] // HD
    befores = (earlier_blocks(soft_key), earlier_blocks(soft_value))
    closing = list(closing_states(lin_key, lin_value, decay_rows, PARTS))
    closing[0], *befores = lax.optimization_barrier((closing[0], *befores))
    incoming = [incoming_states(closing[part], device_logs[part]) for part in range(PARTS)]
    groups = []
    for g in range(kv_count):
        if groups:
            soft_query, groups[-1] = lax.optimization_barrier((soft_query, groups[-1]))
        groups.append(
            softmax_heads(
                place,
                soft_query,
                g * GROUP,
                GROUP,
                (soft_key, g),
                (soft_value, g),
                (befores[0], g),
                (befores[1], g),
            )
        )
    groups = [passed_along(group, "pp", 1) for group in groups]
    for part in range(min(PARTS, kv_count)):
        incoming[part], groups[part] = lax.optimization_barrier((incoming[part], groups[part]))
    arrays = (lin_query, lin_key, lin_value, decay_rows, out_gate, norm_gain)
    chunks = lightning_chunks(place, arrays, incoming)
    soft_handed = joined(groups, soft_query.shape[2])
    return (joined(chunks, lin_query.shape[2]), soft_handed)


def local(
    lin_query, lin_key, lin_value, log_decay, out_gate, norm_gain, soft_query, soft_key, soft_value
):
    arrays = (
        lin_query,
        lin_key,
        lin_value,
        jnp.swapaxes(log_decay, 1, 2),
        out_gate,
        norm_gain,
        soft_query,
        soft_key,
        soft_value,
    )
    arrays = tuple(pltpu.with_memory_space_constraint(x, pltpu.HBM) for x in arrays)
    place = lax.axis_index("ctx").astype(jnp.int32)[None]
    if lax.axis_size("ctx") > 2:
        return ahead(jnp.split(jnp.sum(log_decay, axis=1), PARTS, axis=1), *arrays, place)
    turn = lax.axis_index("tp") & 1
    unused = [None] * PARTS
    return lax.cond(turn == 0, functools.partial(raw_first, unused), functools.partial(worked_out_first, unused), *arrays, place)


def solution(mesh):
    wide = P("pp", "ctx", "tp")
    return jax.shard_map(
        local,
        mesh=mesh,
        in_specs=(wide, wide, wide, wide, wide, P("pp", "tp"), wide, wide, wide),
        out_specs=(wide, wide),
        check_vma=False,
    )
```

```python
import functools

import jax
import jax.numpy as jnp
from jax import lax
from jax.experimental import pallas as pl
from jax.experimental.pallas import tpu as pltpu
from jax.sharding import PartitionSpec as P

HEADS = 64
KV_HEADS = 8
HD = 128
BLK = 256
GROUP = HEADS // KV_HEADS
HALF = BLK // 2

epsilon = 1e-06
lowest = -1e30
LOG2E = 1.4426950408889634
MIB = 1 << 20


def passed_along(block, axis, distance):
    devices = lax.axis_size(axis)
    return lax.ppermute(block, axis, [((i - distance) % devices, i) for i in range(devices)])


def running_sums(decay_rows):
    total = decay_rows
    place = lax.broadcasted_iota(jnp.int32, total.shape, 1)
    reach = 1
    while reach < total.shape[1]:
        total = total + jnp.where(place >= reach, pltpu.roll(total, reach, 1), 0.0)
        reach *= 2
    return total


def turned(rows):
    fill = jnp.zeros((HD - rows.shape[0], rows.shape[1]), rows.dtype)
    return jnp.transpose(jnp.concatenate([rows, fill], axis=0))


def states_kernel(key_ref, value_ref, decay_ref, *state_refs):
    running = running_sums(decay_ref[0])
    press = turned(jnp.exp(running[:, BLK - 1 :] - running))
    states = []
    for h in range(running.shape[0]):
        lanes = slice(h * HD, (h + 1) * HD)
        pressed = (key_ref[0, :, lanes].astype(jnp.float32) * press[:, h : h + 1]).astype(jnp.bfloat16)
        states.append(
            lax.dot_general(
                pressed, value_ref[0, :, lanes], (((0,), (0,)), ((), ())), preferred_element_type=jnp.float32
            )
        )
    for part, state_ref in enumerate(state_refs):

        @pl.when(pl.program_id(0) == part)
        def _(state_ref=state_ref):
            for h, state in enumerate(states):
                state_ref[h] = state.astype(state_ref.dtype)


def closing_states(lin_key, lin_value, decay_rows, parts):
    heads = decay_rows.shape[1] // parts
    wide = pl.BlockSpec((1, BLK, heads * HD), lambda i: (0, 0, i))
    return pl.pallas_call(
        states_kernel,
        grid=(parts,),
        in_specs=[wide, wide, pl.BlockSpec((1, heads, BLK), lambda i: (0, i, 0))],
        out_specs=[pl.BlockSpec((heads, HD, HD), lambda i: (0, 0, 0))] * parts,
        out_shape=[jax.ShapeDtypeStruct((heads, HD, HD), jnp.bfloat16)] * parts,
        compiler_params=pltpu.CompilerParams(vmem_limit_bytes=16 * MIB),
        name="closing_states",
    )(lin_key, lin_value, decay_rows)


def mix_kernel(place_ref, query_ref, key_ref, value_ref, decay_ref, gate_ref, gain_ref, state_ref, *out_refs):
    running = running_sums(decay_ref[0])
    columns = turned(running)
    lift = jnp.exp(columns)
    causal = lax.broadcasted_iota(jnp.int32, (HALF, HALF), 0) >= lax.broadcasted_iota(
        jnp.int32, (HALF, HALF), 1
    )
    turned_dims = (((1,), (1,)), ((), ()))
    owner = []
    for out_ref in out_refs:
        first = len(owner)
        owner += [(out_ref, first)] * (out_ref.shape[2] // HD)
    for h in range(state_ref.shape[0]):
        lanes = slice(h * HD, (h + 1) * HD)
        queries = query_ref[0, :, lanes]
        keys = key_ref[0, :, lanes]
        values = value_ref[0, :, lanes]
        column = columns[:, h : h + 1]
        row = running[h : h + 1, :]
        earlier = jnp.dot(queries, state_ref[h], preferred_element_type=jnp.float32) * lift[:, h : h + 1]
        earlier = jnp.where(place_ref[0] > 0, earlier, 0.0)
        parts = []
        for b in range(2):
            rows = slice(b * HALF, (b + 1) * HALF)
            seen = (b + 1) * HALF
            scores = lax.dot_general(
                queries[rows], keys[:seen], turned_dims, preferred_element_type=jnp.float32
            )
            pieces = []
            for c in range(b + 1):
                span = slice(c * HALF, (c + 1) * HALF)
                gap = column[rows] - row[:, span]
                if c == b:
                    fall = jnp.where(causal, jnp.exp(jnp.where(causal, gap, 0.0)), 0.0)
                else:
                    fall = jnp.exp(gap)
                pieces.append((scores[:, span] * fall).astype(jnp.bfloat16))
            weights = pieces[0] if b == 0 else jnp.concatenate(pieces, axis=1)
            parts.append(jnp.dot(weights, values[:seen], preferred_element_type=jnp.float32))
        mixture = jnp.concatenate(parts, axis=0) + earlier
        scale = lax.rsqrt(jnp.mean(mixture * mixture, axis=1, keepdims=True) + epsilon)
        gate = jax.nn.sigmoid(gate_ref[0, :, lanes].astype(jnp.float32))
        result = mixture * scale * gain_ref[0:1, lanes] * gate
        out_ref, first = owner[h]
        lanes = slice((h - first) * HD, (h - first + 1) * HD)
        out_ref[0, :, lanes] = result.astype(out_ref.dtype)


def lightning(
    place, lin_query, lin_key, lin_value, decay_rows, out_gate, norm_gain, incoming, part, parts, chunks
):
    heads = decay_rows.shape[1] // parts
    wide = pl.BlockSpec((1, BLK, heads * HD), lambda i, place: (0, 0, part))
    return pl.pallas_call(
        mix_kernel,
        grid_spec=pltpu.PrefetchScalarGridSpec(
            num_scalar_prefetch=1,
            grid=(1,),
            in_specs=[
                wide,
                wide,
                wide,
                pl.BlockSpec((1, heads, BLK), lambda i, place: (0, part, 0)),
                wide,
                pl.BlockSpec((1, heads * HD), lambda i, place: (0, part)),
                pl.BlockSpec((heads, HD, HD), lambda i, place: (0, 0, 0)),
            ],
            out_specs=[pl.BlockSpec((1, BLK, n * HD), lambda i, place: (0, 0, 0)) for n in chunks],
        ),
        out_shape=[jax.ShapeDtypeStruct((1, BLK, n * HD), jnp.bfloat16) for n in chunks],
        compiler_params=pltpu.CompilerParams(vmem_limit_bytes=20 * MIB),
        name="lightning_mix",
    )(place, lin_query, lin_key, lin_value, decay_rows, out_gate, norm_gain, incoming)


def copied(pieces, sems):
    copies = [pltpu.make_async_copy(a, b, sems.at[i]) for i, (a, b) in enumerate(pieces)]
    for copy in copies:
        copy.start()
    for copy in copies:
        copy.wait()


def pack_kernel(query_ref, key_ref, value_ref, raw_ref, *refs):
    width = GROUP * HD
    pieces = [
        (query_ref.at[:, :, pl.ds(0, width)], raw_ref.at[:, :, pl.ds(0, width)]),
        (key_ref.at[:, :, pl.ds(0, HD)], raw_ref.at[:, :, pl.ds(width, HD)]),
        (value_ref.at[:, :, pl.ds(0, HD)], raw_ref.at[:, :, pl.ds(width + HD, HD)]),
    ]
    for i, pair_ref in enumerate(refs[:-1]):
        lanes = pl.ds((i + 1) * HD, HD)
        pieces.append((key_ref.at[:, :, lanes], pair_ref.at[:, :, pl.ds(0, HD)]))
        pieces.append((value_ref.at[:, :, lanes], pair_ref.at[:, :, pl.ds(HD, HD)]))
    copied(pieces, refs[-1])


def packed(soft_query, soft_key, soft_value):
    kv_count = soft_key.shape[2] // HD
    widths = [(GROUP + 2) * HD] + [2 * HD] * (kv_count - 1)
    return pl.pallas_call(
        pack_kernel,
        in_specs=[pl.BlockSpec(memory_space=pltpu.HBM)] * 3,
        out_specs=[pl.BlockSpec(memory_space=pltpu.VMEM)] * kv_count,
        out_shape=[pltpu.VMEM((1, BLK, width), jnp.bfloat16) for width in widths],
        scratch_shapes=[pltpu.SemaphoreType.DMA((1 + 2 * kv_count,))],
        compiler_params=pltpu.CompilerParams(vmem_limit_bytes=4 * MIB),
        name="packed",
    )(soft_query, soft_key, soft_value)


def attend(place, query_ref, key_ref, value_ref, before_key_ref, before_value_ref, out_ref):
    others = before_key_ref.shape[0]
    factor = HD ** (-0.5) * LOG2E
    causal = lax.broadcasted_iota(jnp.int32, (BLK, BLK), 0) >= lax.broadcasted_iota(jnp.int32, (BLK, BLK), 1)
    turned_dims = (((1,), (1,)), ((), ()))

    def scored(queries, keys):
        return lax.dot_general(queries, keys, turned_dims, preferred_element_type=jnp.float32)

    for h in range(query_ref.shape[2] // HD):
        lanes = slice(h * HD, (h + 1) * HD)
        queries = query_ref[0, :, lanes]
        own = jnp.where(causal, scored(queries, key_ref[0]), lowest)
        peak = jnp.max(own, axis=1, keepdims=True)
        if others == 1:
            before = jnp.where(place > 0, scored(queries, before_key_ref[0]), lowest)
            peak = jnp.maximum(peak, jnp.max(before, axis=1, keepdims=True))
            own = jnp.exp2((own - peak) * factor)
            before = jnp.exp2((before - peak) * factor)
            totals = jnp.sum(own, axis=1, keepdims=True) + jnp.sum(before, axis=1, keepdims=True)
            weighted = jnp.dot(
                own.astype(jnp.bfloat16), value_ref[0], preferred_element_type=jnp.float32
            ) + jnp.dot(
                before.astype(jnp.bfloat16), before_value_ref[0], preferred_element_type=jnp.float32
            )
        else:
            own = jnp.exp2((own - peak) * factor)
            totals = jnp.sum(own, axis=1, keepdims=True)
            weighted = jnp.dot(
                own.astype(jnp.bfloat16), value_ref[0], preferred_element_type=jnp.float32
            )

            def absorb(turn, kept):
                peak, totals, weighted = kept
                scores = scored(queries, before_key_ref[turn])
                new_peak = jnp.maximum(peak, jnp.max(scores, axis=1, keepdims=True))
                shrink = jnp.exp2((peak - new_peak) * factor)
                scores = jnp.exp2((scores - new_peak) * factor)
                totals = totals * shrink + jnp.sum(scores, axis=1, keepdims=True)
                weighted = weighted * shrink + jnp.dot(
                    scores.astype(jnp.bfloat16),
                    before_value_ref[turn],
                    preferred_element_type=jnp.float32,
                )
                return (new_peak, totals, weighted)

            peak, totals, weighted = lax.fori_loop(0, place, absorb, (peak, totals, weighted))
        out_ref[0, :, lanes] = (weighted / totals).astype(out_ref.dtype)


def soft_kernel(place_ref, query_ref, key_ref, value_ref, before_key_ref, before_value_ref, out_ref):
    attend(place_ref[0], query_ref, key_ref, value_ref, before_key_ref, before_value_ref, out_ref)


def lanes_at(rows, width, index):
    return pl.BlockSpec((rows, BLK, width), lambda i, place: (0, 0, index))


def softmax_heads(place, soft_query, first, count, key, value, before_key, before_value):
    others = before_key[0].shape[0]
    return pl.pallas_call(
        soft_kernel,
        grid_spec=pltpu.PrefetchScalarGridSpec(
            num_scalar_prefetch=1,
            grid=(1,),
            in_specs=[
                lanes_at(1, count * HD, first // count),
                lanes_at(1, HD, key[1]),
                lanes_at(1, HD, value[1]),
                lanes_at(others, HD, before_key[1]),
                lanes_at(others, HD, before_value[1]),
            ],
            out_specs=lanes_at(1, count * HD, 0),
        ),
        out_shape=jax.ShapeDtypeStruct((1, BLK, count * HD), jnp.bfloat16),
        compiler_params=pltpu.CompilerParams(vmem_limit_bytes=20 * MIB),
        name="softmax_heads",
    )(place, soft_query, key[0], value[0], before_key[0], before_value[0])


def softmax_all(place, query, pair, before):
    groups = pair.shape[2] // (2 * HD)
    others = before.shape[0]

    def by_group(rows, width, start=0):
        return pl.BlockSpec((rows, BLK, width), lambda i, place: (0, 0, start + i))

    return pl.pallas_call(
        soft_kernel,
        grid_spec=pltpu.PrefetchScalarGridSpec(
            num_scalar_prefetch=1,
            grid=(groups,),
            in_specs=[
                by_group(1, GROUP * HD),
                by_group(1, HD),
                by_group(1, HD, groups),
                by_group(others, HD),
                by_group(others, HD, groups),
            ],
            out_specs=by_group(1, GROUP * HD),
        ),
        out_shape=pltpu.HBM(query.shape, jnp.bfloat16),
        compiler_params=pltpu.CompilerParams(vmem_limit_bytes=20 * MIB),
        name="softmax_all",
    )(place, query, pair, pair, before, before)


def joined_kernel(key_ref, value_ref, out_ref, sems):
    width = key_ref.shape[2]
    copied(
        [
            (key_ref, out_ref.at[:, :, pl.ds(0, width)]),
            (value_ref, out_ref.at[:, :, pl.ds(width, width)]),
        ],
        sems,
    )


def side_by_side(soft_key, soft_value):
    return pl.pallas_call(
        joined_kernel,
        in_specs=[pl.BlockSpec(memory_space=pltpu.HBM)] * 2,
        out_specs=pl.BlockSpec(memory_space=pltpu.VMEM),
        out_shape=pltpu.VMEM((1, BLK, 2 * soft_key.shape[2]), jnp.bfloat16),
        scratch_shapes=[pltpu.SemaphoreType.DMA((2,))],
        compiler_params=pltpu.CompilerParams(vmem_limit_bytes=2 * MIB),
        name="side_by_side",
    )(soft_key, soft_value)


def finish_kernel(
    place_ref, query_ref, key_ref, value_ref, before_key_ref, before_value_ref, ready_ref, out_ref
):
    here = pl.program_id(0) == 0

    @pl.when(here)
    def _():
        attend(place_ref[0], query_ref, key_ref, value_ref, before_key_ref, before_value_ref, out_ref)

    @pl.when(jnp.logical_not(here))
    def _():
        out_ref[...] = ready_ref[...]


def softmax_finish(place, raw, before, ready):
    others = before.shape[0]
    width = GROUP * HD
    groups = 1 + ready.shape[2] // width
    return pl.pallas_call(
        finish_kernel,
        grid_spec=pltpu.PrefetchScalarGridSpec(
            num_scalar_prefetch=1,
            grid=(groups,),
            in_specs=[
                lanes_at(1, width, 0),
                lanes_at(1, HD, GROUP),
                lanes_at(1, HD, GROUP + 1),
                lanes_at(others, HD, 0),
                lanes_at(others, HD, 1),
                pl.BlockSpec((1, BLK, width), lambda i, place: (0, 0, jnp.maximum(i - 1, 0))),
            ],
            out_specs=pl.BlockSpec((1, BLK, width), lambda i, place: (0, 0, i)),
        ),
        out_shape=pltpu.HBM((1, BLK, groups * width), jnp.bfloat16),
        compiler_params=pltpu.CompilerParams(vmem_limit_bytes=20 * MIB),
        name="softmax_finish",
    )(place, raw, raw, raw, before, before, ready)


def place_kernel(start, block_ref, *refs):
    whole_ref, sems = refs[-2:]
    copied([(block_ref, whole_ref.at[:, :, pl.ds(start, block_ref.shape[2])])], sems)


def placed(block, start, width, whole=None):
    anywhere = pl.BlockSpec(memory_space=pl.ANY)
    in_hbm = pl.BlockSpec(memory_space=pltpu.HBM)
    operands = (block,) if whole is None else (block, whole)
    return pl.pallas_call(
        functools.partial(place_kernel, start),
        in_specs=[anywhere] + [in_hbm] * (len(operands) - 1),
        out_specs=in_hbm,
        out_shape=pltpu.HBM(block.shape[:2] + (width,), block.dtype),
        scratch_shapes=[pltpu.SemaphoreType.DMA((1,))],
        input_output_aliases={} if whole is None else {1: 0},
        compiler_params=pltpu.CompilerParams(vmem_limit_bytes=1 * MIB),
        name="placed",
    )(*operands)


def earlier_blocks(block):
    devices = lax.axis_size("ctx")
    if devices == 2:
        return passed_along(block, "ctx", 1)
    return lax.all_gather(block, "ctx", axis=0, tiled=True)[: devices - 1]


def incoming_states(closing, device_log):
    if lax.axis_size("ctx") == 2:
        return passed_along(closing, "ctx", 1)
    states = lax.all_gather(closing[None], "ctx", axis=0, tiled=True)
    logs = lax.all_gather(device_log, "ctx", axis=0, tiled=True)
    earlier = (lax.iota(jnp.int32, logs.shape[0]) < lax.axis_index("ctx"))[:, None]
    reached = jnp.sum(jnp.where(earlier, logs, 0.0), axis=0)
    rising = jnp.cumsum(logs, axis=0)
    weight = jnp.where(earlier, jnp.exp(jnp.where(earlier, reached[None, :] - rising, 0.0)), 0.0)
    return jnp.sum(weight[:, :, None, None] * states.astype(jnp.float32), axis=0).astype(jnp.bfloat16)


PARTS = 2
LAST = 2


def joined(chunks, width):
    whole = None
    start = 0
    for chunk in chunks:
        whole = placed(chunk, start, width, whole)
        start += chunk.shape[2]
    return whole


def lightning_chunks(place, arrays, incoming):
    heads = incoming[0].shape[0]
    chunks = []
    for part in range(PARTS):
        sizes = [heads - LAST, LAST] if part == PARTS - 1 else [heads]
        chunks += lightning(place, *arrays, incoming[part], part, PARTS, sizes)
    return [passed_along(chunk, "pp", 1) for chunk in chunks]


def ahead(
    device_logs,
    lin_query,
    lin_key,
    lin_value,
    decay_rows,
    out_gate,
    norm_gain,
    soft_query,
    soft_key,
    soft_value,
    place,
):
    raw, *pairs = packed(soft_query, soft_key, soft_value)
    handed_raw = passed_along(raw, "pp", 1)
    befores = [earlier_blocks(pair) for pair in pairs]
    lin_key, lin_value, raw = lax.optimization_barrier((lin_key, lin_value, raw))
    closing = list(closing_states(lin_key, lin_value, decay_rows, PARTS))
    closing[0], *befores = lax.optimization_barrier((closing[0], *befores))
    ready = [
        softmax_heads(
            place, soft_query, (g + 1) * GROUP, GROUP, (pair, 0), (pair, 1), (before, 0), (before, 1)
        )
        for g, (pair, before) in enumerate(zip(pairs, befores))
    ]
    incoming = [incoming_states(closing[part], device_logs[part]) for part in range(PARTS)]
    ready = [passed_along(group, "pp", 1) for group in ready]
    ready = ready[0] if len(ready) == 1 else jnp.concatenate(ready, axis=2)
    incoming[0], handed_raw = lax.optimization_barrier((incoming[0], handed_raw))
    arrays = (lin_query, lin_key, lin_value, decay_rows, out_gate, norm_gain)
    chunks = lightning_chunks(place, arrays, incoming)
    before = earlier_blocks(handed_raw[:, :, GROUP * HD :])
    soft_handed = softmax_finish(place, handed_raw, before, ready)
    return (joined(chunks, lin_query.shape[2]), soft_handed)


def raw_first(
    device_logs,
    lin_query,
    lin_key,
    lin_value,
    decay_rows,
    out_gate,
    norm_gain,
    soft_query,
    soft_key,
    soft_value,
    place,
):
    handed_query = passed_along(soft_query, "pp", 1)
    pair = side_by_side(soft_key, soft_value)
    lin_key, lin_value, pair = lax.optimization_barrier((lin_key, lin_value, pair))
    handed_pair = passed_along(pair, "pp", 1)
    closing = closing_states(lin_key, lin_value, decay_rows, PARTS)
    incoming = [incoming_states(closing[part], device_logs[part]) for part in range(PARTS)]
    incoming[-1], handed_query, handed_pair = lax.optimization_barrier((incoming[-1], handed_query, handed_pair))
    arrays = (lin_query, lin_key, lin_value, decay_rows, out_gate, norm_gain)
    chunks = lightning_chunks(place, arrays, incoming)
    soft_handed = softmax_all(place, handed_query, handed_pair, earlier_blocks(handed_pair))
    return (joined(chunks, lin_query.shape[2]), soft_handed)


def worked_out_first(
    device_logs,
    lin_query,
    lin_key,
    lin_value,
    decay_rows,
    out_gate,
    norm_gain,
    soft_query,
    soft_key,
    soft_value,
    place,
):
    kv_count = soft_key.shape[2] // HD
    befores = (earlier_blocks(soft_key), earlier_blocks(soft_value))
    closing = list(closing_states(lin_key, lin_value, decay_rows, PARTS))
    closing[0], *befores = lax.optimization_barrier((closing[0], *befores))
    befores = [pltpu.with_memory_space_constraint(before, pltpu.VMEM) for before in befores]
    incoming = [incoming_states(closing[part], device_logs[part]) for part in range(PARTS)]
    groups = []
    for g in range(kv_count):
        if groups:
            soft_query, groups[-1] = lax.optimization_barrier((soft_query, groups[-1]))
        groups.append(
            softmax_heads(
                place,
                soft_query,
                g * GROUP,
                GROUP,
                (soft_key, g),
                (soft_value, g),
                (befores[0], g),
                (befores[1], g),
            )
        )
    groups = [passed_along(group, "pp", 1) for group in groups]
    for part in range(min(PARTS, kv_count)):
        incoming[part], groups[part] = lax.optimization_barrier((incoming[part], groups[part]))
    arrays = (lin_query, lin_key, lin_value, decay_rows, out_gate, norm_gain)
    chunks = lightning_chunks(place, arrays, incoming)
    soft_handed = joined(groups, soft_query.shape[2])
    return (joined(chunks, lin_query.shape[2]), soft_handed)


def local(
    lin_query, lin_key, lin_value, log_decay, out_gate, norm_gain, soft_query, soft_key, soft_value
):
    arrays = (
        lin_query,
        lin_key,
        lin_value,
        jnp.swapaxes(log_decay, 1, 2),
        out_gate,
        norm_gain,
        soft_query,
        soft_key,
        soft_value,
    )
    arrays = tuple(pltpu.with_memory_space_constraint(x, pltpu.HBM) for x in arrays)
    place = lax.axis_index("ctx").astype(jnp.int32)[None]
    if lax.axis_size("ctx") > 2:
        return ahead(jnp.split(jnp.sum(log_decay, axis=1), PARTS, axis=1), *arrays, place)
    turn = lax.axis_index("tp") & 1
    unused = [None] * PARTS
    return lax.cond(turn == 0, functools.partial(raw_first, unused), functools.partial(worked_out_first, unused), *arrays, place)


def solution(mesh):
    wide = P("pp", "ctx", "tp")
    return jax.shard_map(
        local,
        mesh=mesh,
        in_specs=(wide, wide, wide, wide, wide, P("pp", "tp"), wide, wide, wide),
        out_specs=(wide, wide),
        check_vma=False,
    )
```

```python
import functools

import jax
import jax.numpy as jnp
from jax import lax
from jax.experimental import pallas as pl
from jax.experimental.pallas import tpu as pltpu
from jax.sharding import PartitionSpec as P

HEADS = 64
KV_HEADS = 8
HD = 128
BLK = 256
GROUP = HEADS // KV_HEADS
HALF = BLK // 2

epsilon = 1e-06
lowest = -1e30
LOG2E = 1.4426950408889634
MIB = 1 << 20


def passed_along(block, axis, distance):
    devices = lax.axis_size(axis)
    return lax.ppermute(block, axis, [((i - distance) % devices, i) for i in range(devices)])


def running_sums(decay_rows):
    total = decay_rows
    place = lax.broadcasted_iota(jnp.int32, total.shape, 1)
    reach = 1
    while reach < total.shape[1]:
        total = total + jnp.where(place >= reach, pltpu.roll(total, reach, 1), 0.0)
        reach *= 2
    return total


def turned(rows):
    fill = jnp.zeros((HD - rows.shape[0], rows.shape[1]), rows.dtype)
    return jnp.transpose(jnp.concatenate([rows, fill], axis=0))


def states_kernel(key_ref, value_ref, decay_ref, *state_refs):
    running = running_sums(decay_ref[0])
    press = turned(jnp.exp(running[:, BLK - 1 :] - running))
    states = []
    for h in range(running.shape[0]):
        lanes = slice(h * HD, (h + 1) * HD)
        pressed = (key_ref[0, :, lanes].astype(jnp.float32) * press[:, h : h + 1]).astype(jnp.bfloat16)
        states.append(
            lax.dot_general(
                pressed, value_ref[0, :, lanes], (((0,), (0,)), ((), ())), preferred_element_type=jnp.float32
            )
        )
    for part, state_ref in enumerate(state_refs):

        @pl.when(pl.program_id(0) == part)
        def _(state_ref=state_ref):
            for h, state in enumerate(states):
                state_ref[h] = state.astype(state_ref.dtype)


def closing_states(lin_key, lin_value, decay_rows, parts):
    heads = decay_rows.shape[1] // parts
    wide = pl.BlockSpec((1, BLK, heads * HD), lambda i: (0, 0, i))
    return pl.pallas_call(
        states_kernel,
        grid=(parts,),
        in_specs=[wide, wide, pl.BlockSpec((1, heads, BLK), lambda i: (0, i, 0))],
        out_specs=[pl.BlockSpec((heads, HD, HD), lambda i: (0, 0, 0))] * parts,
        out_shape=[jax.ShapeDtypeStruct((heads, HD, HD), jnp.bfloat16)] * parts,
        compiler_params=pltpu.CompilerParams(vmem_limit_bytes=16 * MIB),
        name="closing_states",
    )(lin_key, lin_value, decay_rows)


def mix_kernel(place_ref, query_ref, key_ref, value_ref, decay_ref, gate_ref, gain_ref, state_ref, *out_refs):
    running = running_sums(decay_ref[0])
    columns = turned(running)
    lift = jnp.exp(columns)
    causal = lax.broadcasted_iota(jnp.int32, (HALF, HALF), 0) >= lax.broadcasted_iota(
        jnp.int32, (HALF, HALF), 1
    )
    turned_dims = (((1,), (1,)), ((), ()))
    owner = []
    for out_ref in out_refs:
        first = len(owner)
        owner += [(out_ref, first)] * (out_ref.shape[2] // HD)
    for h in range(state_ref.shape[0]):
        lanes = slice(h * HD, (h + 1) * HD)
        queries = query_ref[0, :, lanes]
        keys = key_ref[0, :, lanes]
        values = value_ref[0, :, lanes]
        column = columns[:, h : h + 1]
        row = running[h : h + 1, :]
        earlier = jnp.dot(queries, state_ref[h], preferred_element_type=jnp.float32) * lift[:, h : h + 1]
        earlier = jnp.where(place_ref[0] > 0, earlier, 0.0)
        parts = []
        for b in range(2):
            rows = slice(b * HALF, (b + 1) * HALF)
            seen = (b + 1) * HALF
            scores = lax.dot_general(
                queries[rows], keys[:seen], turned_dims, preferred_element_type=jnp.float32
            )
            pieces = []
            for c in range(b + 1):
                span = slice(c * HALF, (c + 1) * HALF)
                gap = column[rows] - row[:, span]
                if c == b:
                    fall = jnp.where(causal, jnp.exp(jnp.where(causal, gap, 0.0)), 0.0)
                else:
                    fall = jnp.exp(gap)
                pieces.append((scores[:, span] * fall).astype(jnp.bfloat16))
            weights = pieces[0] if b == 0 else jnp.concatenate(pieces, axis=1)
            parts.append(jnp.dot(weights, values[:seen], preferred_element_type=jnp.float32))
        mixture = jnp.concatenate(parts, axis=0) + earlier
        scale = lax.rsqrt(jnp.mean(mixture * mixture, axis=1, keepdims=True) + epsilon)
        gate = jax.nn.sigmoid(gate_ref[0, :, lanes].astype(jnp.float32))
        result = mixture * scale * gain_ref[0:1, lanes] * gate
        out_ref, first = owner[h]
        lanes = slice((h - first) * HD, (h - first + 1) * HD)
        out_ref[0, :, lanes] = result.astype(out_ref.dtype)


def lightning(
    place, lin_query, lin_key, lin_value, decay_rows, out_gate, norm_gain, incoming, part, parts, chunks
):
    heads = decay_rows.shape[1] // parts
    wide = pl.BlockSpec((1, BLK, heads * HD), lambda i, place: (0, 0, part))
    return pl.pallas_call(
        mix_kernel,
        grid_spec=pltpu.PrefetchScalarGridSpec(
            num_scalar_prefetch=1,
            grid=(1,),
            in_specs=[
                wide,
                wide,
                wide,
                pl.BlockSpec((1, heads, BLK), lambda i, place: (0, part, 0)),
                wide,
                pl.BlockSpec((1, heads * HD), lambda i, place: (0, part)),
                pl.BlockSpec((heads, HD, HD), lambda i, place: (0, 0, 0)),
            ],
            out_specs=[pl.BlockSpec((1, BLK, n * HD), lambda i, place: (0, 0, 0)) for n in chunks],
        ),
        out_shape=[jax.ShapeDtypeStruct((1, BLK, n * HD), jnp.bfloat16) for n in chunks],
        compiler_params=pltpu.CompilerParams(vmem_limit_bytes=20 * MIB),
        name="lightning_mix",
    )(place, lin_query, lin_key, lin_value, decay_rows, out_gate, norm_gain, incoming)


def copied(pieces, sems):
    copies = [pltpu.make_async_copy(a, b, sems.at[i]) for i, (a, b) in enumerate(pieces)]
    for copy in copies:
        copy.start()
    for copy in copies:
        copy.wait()


def pack_kernel(query_ref, key_ref, value_ref, raw_ref, *refs):
    width = GROUP * HD
    pieces = [
        (query_ref.at[:, :, pl.ds(0, width)], raw_ref.at[:, :, pl.ds(0, width)]),
        (key_ref.at[:, :, pl.ds(0, HD)], raw_ref.at[:, :, pl.ds(width, HD)]),
        (value_ref.at[:, :, pl.ds(0, HD)], raw_ref.at[:, :, pl.ds(width + HD, HD)]),
    ]
    for i, pair_ref in enumerate(refs[:-1]):
        lanes = pl.ds((i + 1) * HD, HD)
        pieces.append((key_ref.at[:, :, lanes], pair_ref.at[:, :, pl.ds(0, HD)]))
        pieces.append((value_ref.at[:, :, lanes], pair_ref.at[:, :, pl.ds(HD, HD)]))
    copied(pieces, refs[-1])


def packed(soft_query, soft_key, soft_value):
    kv_count = soft_key.shape[2] // HD
    widths = [(GROUP + 2) * HD] + [2 * HD] * (kv_count - 1)
    return pl.pallas_call(
        pack_kernel,
        in_specs=[pl.BlockSpec(memory_space=pltpu.HBM)] * 3,
        out_specs=[pl.BlockSpec(memory_space=pltpu.VMEM)] * kv_count,
        out_shape=[pltpu.VMEM((1, BLK, width), jnp.bfloat16) for width in widths],
        scratch_shapes=[pltpu.SemaphoreType.DMA((1 + 2 * kv_count,))],
        compiler_params=pltpu.CompilerParams(vmem_limit_bytes=4 * MIB),
        name="packed",
    )(soft_query, soft_key, soft_value)


def attend(place, query_ref, key_ref, value_ref, before_key_ref, before_value_ref, out_ref):
    others = before_key_ref.shape[0]
    factor = HD ** (-0.5) * LOG2E
    causal = lax.broadcasted_iota(jnp.int32, (BLK, BLK), 0) >= lax.broadcasted_iota(jnp.int32, (BLK, BLK), 1)
    turned_dims = (((1,), (1,)), ((), ()))

    def scored(queries, keys):
        return lax.dot_general(queries, keys, turned_dims, preferred_element_type=jnp.float32)

    for h in range(query_ref.shape[2] // HD):
        lanes = slice(h * HD, (h + 1) * HD)
        queries = query_ref[0, :, lanes]
        own = jnp.where(causal, scored(queries, key_ref[0]), lowest)
        peak = jnp.max(own, axis=1, keepdims=True)
        if others == 1:
            before = jnp.where(place > 0, scored(queries, before_key_ref[0]), lowest)
            peak = jnp.maximum(peak, jnp.max(before, axis=1, keepdims=True))
            own = jnp.exp2((own - peak) * factor)
            before = jnp.exp2((before - peak) * factor)
            totals = jnp.sum(own, axis=1, keepdims=True) + jnp.sum(before, axis=1, keepdims=True)
            weighted = jnp.dot(
                own.astype(jnp.bfloat16), value_ref[0], preferred_element_type=jnp.float32
            ) + jnp.dot(
                before.astype(jnp.bfloat16), before_value_ref[0], preferred_element_type=jnp.float32
            )
        else:
            own = jnp.exp2((own - peak) * factor)
            totals = jnp.sum(own, axis=1, keepdims=True)
            weighted = jnp.dot(
                own.astype(jnp.bfloat16), value_ref[0], preferred_element_type=jnp.float32
            )

            def absorb(turn, kept):
                peak, totals, weighted = kept
                scores = scored(queries, before_key_ref[turn])
                new_peak = jnp.maximum(peak, jnp.max(scores, axis=1, keepdims=True))
                shrink = jnp.exp2((peak - new_peak) * factor)
                scores = jnp.exp2((scores - new_peak) * factor)
                totals = totals * shrink + jnp.sum(scores, axis=1, keepdims=True)
                weighted = weighted * shrink + jnp.dot(
                    scores.astype(jnp.bfloat16),
                    before_value_ref[turn],
                    preferred_element_type=jnp.float32,
                )
                return (new_peak, totals, weighted)

            peak, totals, weighted = lax.fori_loop(0, place, absorb, (peak, totals, weighted))
        out_ref[0, :, lanes] = (weighted / totals).astype(out_ref.dtype)


def soft_kernel(place_ref, query_ref, key_ref, value_ref, before_key_ref, before_value_ref, out_ref):
    attend(place_ref[0], query_ref, key_ref, value_ref, before_key_ref, before_value_ref, out_ref)


def lanes_at(rows, width, index):
    return pl.BlockSpec((rows, BLK, width), lambda i, place: (0, 0, index))


def softmax_heads(place, soft_query, first, count, key, value, before_key, before_value):
    others = before_key[0].shape[0]
    return pl.pallas_call(
        soft_kernel,
        grid_spec=pltpu.PrefetchScalarGridSpec(
            num_scalar_prefetch=1,
            grid=(1,),
            in_specs=[
                lanes_at(1, count * HD, first // count),
                lanes_at(1, HD, key[1]),
                lanes_at(1, HD, value[1]),
                lanes_at(others, HD, before_key[1]),
                lanes_at(others, HD, before_value[1]),
            ],
            out_specs=lanes_at(1, count * HD, 0),
        ),
        out_shape=jax.ShapeDtypeStruct((1, BLK, count * HD), jnp.bfloat16),
        compiler_params=pltpu.CompilerParams(vmem_limit_bytes=20 * MIB),
        name="softmax_heads",
    )(place, soft_query, key[0], value[0], before_key[0], before_value[0])


def softmax_all(place, query, pair, before):
    groups = pair.shape[2] // (2 * HD)
    others = before.shape[0]

    def by_group(rows, width, start=0):
        return pl.BlockSpec((rows, BLK, width), lambda i, place: (0, 0, start + i))

    return pl.pallas_call(
        soft_kernel,
        grid_spec=pltpu.PrefetchScalarGridSpec(
            num_scalar_prefetch=1,
            grid=(groups,),
            in_specs=[
                by_group(1, GROUP * HD),
                by_group(1, HD),
                by_group(1, HD, groups),
                by_group(others, HD),
                by_group(others, HD, groups),
            ],
            out_specs=by_group(1, GROUP * HD),
        ),
        out_shape=pltpu.HBM(query.shape, jnp.bfloat16),
        compiler_params=pltpu.CompilerParams(vmem_limit_bytes=20 * MIB),
        name="softmax_all",
    )(place, query, pair, pair, before, before)


def joined_kernel(key_ref, value_ref, out_ref, sems):
    width = key_ref.shape[2]
    copied(
        [
            (key_ref, out_ref.at[:, :, pl.ds(0, width)]),
            (value_ref, out_ref.at[:, :, pl.ds(width, width)]),
        ],
        sems,
    )


def side_by_side(soft_key, soft_value):
    return pl.pallas_call(
        joined_kernel,
        in_specs=[pl.BlockSpec(memory_space=pltpu.HBM)] * 2,
        out_specs=pl.BlockSpec(memory_space=pltpu.VMEM),
        out_shape=pltpu.VMEM((1, BLK, 2 * soft_key.shape[2]), jnp.bfloat16),
        scratch_shapes=[pltpu.SemaphoreType.DMA((2,))],
        compiler_params=pltpu.CompilerParams(vmem_limit_bytes=2 * MIB),
        name="side_by_side",
    )(soft_key, soft_value)


def finish_kernel(
    place_ref, query_ref, key_ref, value_ref, before_key_ref, before_value_ref, ready_ref, out_ref
):
    here = pl.program_id(0) == 0

    @pl.when(here)
    def _():
        attend(place_ref[0], query_ref, key_ref, value_ref, before_key_ref, before_value_ref, out_ref)

    @pl.when(jnp.logical_not(here))
    def _():
        out_ref[...] = ready_ref[...]


def softmax_finish(place, raw, before, ready):
    others = before.shape[0]
    width = GROUP * HD
    groups = 1 + ready.shape[2] // width
    return pl.pallas_call(
        finish_kernel,
        grid_spec=pltpu.PrefetchScalarGridSpec(
            num_scalar_prefetch=1,
            grid=(groups,),
            in_specs=[
                lanes_at(1, width, 0),
                lanes_at(1, HD, GROUP),
                lanes_at(1, HD, GROUP + 1),
                lanes_at(others, HD, 0),
                lanes_at(others, HD, 1),
                pl.BlockSpec((1, BLK, width), lambda i, place: (0, 0, jnp.maximum(i - 1, 0))),
            ],
            out_specs=pl.BlockSpec((1, BLK, width), lambda i, place: (0, 0, i)),
        ),
        out_shape=pltpu.HBM((1, BLK, groups * width), jnp.bfloat16),
        compiler_params=pltpu.CompilerParams(vmem_limit_bytes=20 * MIB),
        name="softmax_finish",
    )(place, raw, raw, raw, before, before, ready)


def place_kernel(start, block_ref, *refs):
    whole_ref, sems = refs[-2:]
    copied([(block_ref, whole_ref.at[:, :, pl.ds(start, block_ref.shape[2])])], sems)


def placed(block, start, width, whole=None):
    anywhere = pl.BlockSpec(memory_space=pl.ANY)
    in_hbm = pl.BlockSpec(memory_space=pltpu.HBM)
    operands = (block,) if whole is None else (block, whole)
    return pl.pallas_call(
        functools.partial(place_kernel, start),
        in_specs=[anywhere] + [in_hbm] * (len(operands) - 1),
        out_specs=in_hbm,
        out_shape=pltpu.HBM(block.shape[:2] + (width,), block.dtype),
        scratch_shapes=[pltpu.SemaphoreType.DMA((1,))],
        input_output_aliases={} if whole is None else {1: 0},
        compiler_params=pltpu.CompilerParams(vmem_limit_bytes=1 * MIB),
        name="placed",
    )(*operands)


def earlier_blocks(block):
    devices = lax.axis_size("ctx")
    if devices == 2:
        return passed_along(block, "ctx", 1)
    return lax.all_gather(block, "ctx", axis=0, tiled=True)[: devices - 1]


def incoming_states(closing, device_log):
    if lax.axis_size("ctx") == 2:
        return passed_along(closing, "ctx", 1)
    states = lax.all_gather(closing[None], "ctx", axis=0, tiled=True)
    logs = lax.all_gather(device_log, "ctx", axis=0, tiled=True)
    earlier = (lax.iota(jnp.int32, logs.shape[0]) < lax.axis_index("ctx"))[:, None]
    reached = jnp.sum(jnp.where(earlier, logs, 0.0), axis=0)
    rising = jnp.cumsum(logs, axis=0)
    weight = jnp.where(earlier, jnp.exp(jnp.where(earlier, reached[None, :] - rising, 0.0)), 0.0)
    return jnp.sum(weight[:, :, None, None] * states.astype(jnp.float32), axis=0).astype(jnp.bfloat16)


PARTS = 2
LAST = 2


def joined(chunks, width):
    whole = None
    start = 0
    for chunk in chunks:
        whole = placed(chunk, start, width, whole)
        start += chunk.shape[2]
    return whole


def lightning_chunks(place, arrays, incoming):
    heads = incoming[0].shape[0]
    chunks = []
    for part in range(PARTS):
        sizes = [heads - LAST, LAST] if part == PARTS - 1 else [heads]
        chunks += lightning(place, *arrays, incoming[part], part, PARTS, sizes)
    return [passed_along(chunk, "pp", 1) for chunk in chunks]


def ahead(
    device_logs,
    lin_query,
    lin_key,
    lin_value,
    decay_rows,
    out_gate,
    norm_gain,
    soft_query,
    soft_key,
    soft_value,
    place,
):
    raw, *pairs = packed(soft_query, soft_key, soft_value)
    handed_raw = passed_along(raw, "pp", 1)
    befores = [earlier_blocks(pair) for pair in pairs]
    lin_key, lin_value, raw = lax.optimization_barrier((lin_key, lin_value, raw))
    closing = list(closing_states(lin_key, lin_value, decay_rows, PARTS))
    closing[0], *befores = lax.optimization_barrier((closing[0], *befores))
    ready = [
        softmax_heads(
            place, soft_query, (g + 1) * GROUP, GROUP, (pair, 0), (pair, 1), (before, 0), (before, 1)
        )
        for g, (pair, before) in enumerate(zip(pairs, befores))
    ]
    incoming = [incoming_states(closing[part], device_logs[part]) for part in range(PARTS)]
    ready = [passed_along(group, "pp", 1) for group in ready]
    ready = ready[0] if len(ready) == 1 else jnp.concatenate(ready, axis=2)
    incoming[0], handed_raw = lax.optimization_barrier((incoming[0], handed_raw))
    arrays = (lin_query, lin_key, lin_value, decay_rows, out_gate, norm_gain)
    chunks = lightning_chunks(place, arrays, incoming)
    before = earlier_blocks(handed_raw[:, :, GROUP * HD :])
    soft_handed = softmax_finish(place, handed_raw, before, ready)
    return (joined(chunks, lin_query.shape[2]), soft_handed)


def raw_first(
    device_logs,
    lin_query,
    lin_key,
    lin_value,
    decay_rows,
    out_gate,
    norm_gain,
    soft_query,
    soft_key,
    soft_value,
    place,
):
    handed_query = passed_along(soft_query, "pp", 1)
    pair = side_by_side(soft_key, soft_value)
    lin_key, lin_value, pair = lax.optimization_barrier((lin_key, lin_value, pair))
    handed_pair = passed_along(pair, "pp", 1)
    closing = closing_states(lin_key, lin_value, decay_rows, PARTS)
    incoming = [incoming_states(closing[part], device_logs[part]) for part in range(PARTS)]
    incoming[-1], handed_query, handed_pair = lax.optimization_barrier((incoming[-1], handed_query, handed_pair))
    arrays = (lin_query, lin_key, lin_value, decay_rows, out_gate, norm_gain)
    chunks = lightning_chunks(place, arrays, incoming)
    soft_handed = softmax_all(place, handed_query, handed_pair, earlier_blocks(handed_pair))
    return (joined(chunks, lin_query.shape[2]), soft_handed)


def worked_out_first(
    device_logs,
    lin_query,
    lin_key,
    lin_value,
    decay_rows,
    out_gate,
    norm_gain,
    soft_query,
    soft_key,
    soft_value,
    place,
):
    kv_count = soft_key.shape[2] // HD
    befores = (earlier_blocks(soft_key), earlier_blocks(soft_value))
    closing = list(closing_states(lin_key, lin_value, decay_rows, PARTS))
    closing[0], *befores = lax.optimization_barrier((closing[0], *befores))
    befores = [pltpu.with_memory_space_constraint(before, pltpu.VMEM) for before in befores]
    incoming = [incoming_states(closing[part], device_logs[part]) for part in range(PARTS)]
    groups = []
    for g in range(kv_count):
        if groups:
            soft_query, groups[-1] = lax.optimization_barrier((soft_query, groups[-1]))
        groups.append(
            softmax_heads(
                place,
                soft_query,
                g * GROUP,
                GROUP,
                (soft_key, g),
                (soft_value, g),
                (befores[0], g),
                (befores[1], g),
            )
        )
    groups = [passed_along(group, "pp", 1) for group in groups]
    incoming[0], groups[0] = lax.optimization_barrier((incoming[0], groups[0]))
    arrays = (lin_query, lin_key, lin_value, decay_rows, out_gate, norm_gain)
    chunks = lightning_chunks(place, arrays, incoming)
    soft_handed = joined(groups, soft_query.shape[2])
    return (joined(chunks, lin_query.shape[2]), soft_handed)


def local(
    lin_query, lin_key, lin_value, log_decay, out_gate, norm_gain, soft_query, soft_key, soft_value
):
    arrays = (
        lin_query,
        lin_key,
        lin_value,
        jnp.swapaxes(log_decay, 1, 2),
        out_gate,
        norm_gain,
        soft_query,
        soft_key,
        soft_value,
    )
    arrays = tuple(pltpu.with_memory_space_constraint(x, pltpu.HBM) for x in arrays)
    place = lax.axis_index("ctx").astype(jnp.int32)[None]
    if lax.axis_size("ctx") > 2:
        return ahead(jnp.split(jnp.sum(log_decay, axis=1), PARTS, axis=1), *arrays, place)
    turn = lax.axis_index("tp") & 1
    unused = [None] * PARTS
    return lax.cond(turn == 0, functools.partial(raw_first, unused), functools.partial(worked_out_first, unused), *arrays, place)


def solution(mesh):
    wide = P("pp", "ctx", "tp")
    return jax.shard_map(
        local,
        mesh=mesh,
        in_specs=(wide, wide, wide, wide, wide, P("pp", "tp"), wide, wide, wide),
        out_specs=(wide, wide),
        check_vma=False,
    )
```
